32 devices in a mesh: dp: 4 (over y, core), fsdp: 8 (over z, x).
Axes of the slice: x: 2, y: 2, z: 4, core: 2. Of those that a mesh axis runs over, the one named last changes fastest.
Arguments:
- signal: bfloat16 [256, 64, 4096], P(('dp', 'fsdp')), may hold values from -6 to 6
- segments: int32 [256, 4096], P(('dp', 'fsdp')), may hold values from 0 to 3, never falling along the last dimension, each value on 1 to 2048 neighbouring positions
- cotangent: bfloat16 [256, 32, 8192], P(('dp', 'fsdp')), may hold values from -6 to 6
- upsample_direction: bfloat16 [64, 128], P('dp', 'fsdp'), may hold values from -0.5 to 0.5
- upsample_gain: bfloat16 [64], P('fsdp'), may hold values from 0.5 to 2
- upsample_bias: bfloat16 [32], P('fsdp'), may hold values from -1.5 to 1.5
- dilated_direction: bfloat16 [3, 32, 96], P(None, 'dp', 'fsdp'), may hold values from -0.625 to 0.625
- paired_direction: bfloat16 [3, 2, 32, 32], P(None, None, 'dp', 'fsdp'), may hold values from -1 to 1
- residual_gain: bfloat16 [3, 3, 32], P(None, None, 'fsdp'), may hold values from 0.3984375 to 1.1953125
- residual_bias: bfloat16 [3, 3, 32], P(None, None, 'fsdp'), may hold values from -1.5 to 1.5
Outputs:
- output: bfloat16 [256, 32, 8192], P(('dp', 'fsdp'))
- signal_grad: bfloat16 [256, 64, 4096], P(('dp', 'fsdp'))
- up_dir_grad: float32 [64, 128], P('dp', 'fsdp')
- up_gain_grad: float32 [64], P('fsdp')
- up_bias_grad: float32 [32], P('fsdp')
- dil_dir_grad: float32 [3, 32, 96], P(None, 'dp', 'fsdp')
- pair_dir_grad: float32 [3, 2, 32, 32], P(None, None, 'dp', 'fsdp')
- res_gain_grad: float32 [3, 3, 32], P(None, None, 'fsdp')
- res_bias_grad: float32 [3, 3, 32], P(None, None, 'fsdp')
The draws below stay inside these ranges and needn't reach their ends.
Inputs may be any that keep to these rules, and one draw needn't show every extreme that they name: `segments`: utterance numbers never fall along a row; each utterance is 1 to 2048 input samples long, one exactly that long.
All inputs are finite; a program needn't handle non-finite values.
Results may differ from the reference program's by a relative error of at most 0.017.
Values may be sent and summed in bfloat16 or wider, within the bound.
A program may use at most 384 MiB of HBM per device.

```python
import math
import jax
import jax.numpy as jnp
import numpy as np
from jax import lax

C_IN = 64
CHANNELS_OUT = 32
KERNEL = 4
RESIDUAL_BLOCKS = 3
SEGS = 4
FRAMES = 4096
PACKS = 256


def block_scale(rng, shape, cuts, low, largest):
    loudness, own = 1.0, jax.random.fold_in(rng, 6)
    for position, shards_of in cuts:
        heights = jnp.exp(jax.random.uniform(jax.random.fold_in(own, position), (shards_of,), jnp.float32, low / len(cuts), largest / len(cuts)))
        loudness = loudness * jnp.repeat(heights, shape[position] // shards_of).reshape([-1 if axis == position else 1 for axis in range(len(shape))])
    return loudness


def length_profile(number_of, total, most, lean):
    portions = [(1 << 20) // math.isqrt(standing ** lean) + 1 for standing in range(2, number_of + 1)]
    spare, holding = total - most - (number_of - 1), [1] * (number_of - 1)
    while spare > 0:
        candidates = [i for i in range(number_of - 1) if holding[i] < most]
        whole, remaining = sum([portions[i] for i in candidates]), spare
        for i in candidates:
            addition = min(most - holding[i], max(1, remaining * portions[i] // whole), spare)
            holding[i] = holding[i] + addition
            spare = spare - addition
    return np.array([most] + holding)


def uneven(own_key, amount, total, limit, skew):
    if amount == 2:
        one = jax.random.randint(own_key, (), max(1, total - limit), min(limit, total - 1) + 1)
        return jnp.stack([one, total - one])
    sizes = jnp.asarray(length_profile(amount, total, limit, skew), jnp.int32)
    pairs = (amount - 1) // 2
    source_of, taker = sizes[1:1 + 2 * pairs:2], sizes[2:2 + 2 * pairs:2]
    room = jnp.minimum(source_of - 1, limit - taker)
    moved = jax.random.randint(jax.random.fold_in(own_key, 1), (pairs,), 0, 1 << 20) % (room + 1)
    sizes = sizes.at[1:1 + 2 * pairs:2].set(source_of - moved).at[2:2 + 2 * pairs:2].set(taker + moved)
    return sizes[jax.random.permutation(jax.random.fold_in(own_key, 2), amount)]


def bell_draw(own_key, extent, deviation, most, split=(), kind=jnp.bfloat16):
    entries = jax.random.normal(own_key, extent, jnp.float32) * deviation
    if len(split) > 0:
        entries = block_scale(own_key, extent, split, -0.22, 0.18) * entries
    return jnp.clip(entries, min=-most, max=most).astype(kind)


def setup_inputs(seed: int = 0) -> dict:
    splits = jax.random.split(jax.random.key(seed), 11)
    signal = bell_draw(splits[0], (PACKS, C_IN, FRAMES), 1.0, 6.0, ((0, 32),))
    segments = jax.vmap(lambda own: jnp.searchsorted(jnp.cumsum(uneven(own, SEGS, FRAMES, FRAMES // 2, 0)), jnp.arange(FRAMES), side="right"))(jax.random.split(splits[1], PACKS)).reshape((PACKS, FRAMES)).astype(jnp.int32)
    cotangent = bell_draw(splits[2], (PACKS, CHANNELS_OUT, 2 * FRAMES), 1.0, 6.0, ((0, 32),))
    upsample_direction = bell_draw(splits[3], (C_IN, KERNEL * CHANNELS_OUT), (KERNEL * CHANNELS_OUT) ** -0.5, 0.5, ((0, 4), (1, 8)))
    upsample_gain = jnp.clip(jnp.exp(math.log(2.0) - 1.3862944 * jax.random.uniform(splits[4], (C_IN,), jnp.float32) ** block_scale(splits[4], (C_IN,), ((0, 8),), -0.2, 0.2)), 0.5, 2.0).astype(jnp.bfloat16)
    upsample_bias = bell_draw(splits[5], (CHANNELS_OUT,), 0.3, 1.5, ((0, 8),))
    dilated_direction = bell_draw(splits[6], (RESIDUAL_BLOCKS, CHANNELS_OUT, 3 * CHANNELS_OUT), (3 * CHANNELS_OUT) ** -0.5, 0.625, ((1, 4), (2, 8)))
    paired_direction = bell_draw(splits[7], (RESIDUAL_BLOCKS, 2, CHANNELS_OUT, CHANNELS_OUT), CHANNELS_OUT ** -0.5, 1.0, ((2, 4), (3, 8)))
    residual_gain = jnp.clip(jnp.exp(math.log(1.1953125) - 1.0986123 * jax.random.uniform(splits[8], (RESIDUAL_BLOCKS, 3, CHANNELS_OUT), jnp.float32) ** block_scale(splits[8], (RESIDUAL_BLOCKS, 3, CHANNELS_OUT), ((2, 8),), -0.2, 0.2)), 0.3984375, 1.1953125).astype(jnp.bfloat16)
    residual_bias = bell_draw(splits[9], (RESIDUAL_BLOCKS, 3, CHANNELS_OUT), 0.3, 1.5, ((2, 8),))
    return dict(signal=signal, segments=segments, cotangent=cotangent, upsample_direction=upsample_direction, upsample_gain=upsample_gain, upsample_bias=upsample_bias, dilated_direction=dilated_direction, paired_direction=paired_direction, residual_gain=residual_gain, residual_bias=residual_bias)


@jax.custom_vjp
def reduced_precision(v):
    return lax.optimization_barrier(v.astype(jnp.bfloat16)).astype(jnp.float32)

@jax.custom_vjp
def reduced_backward(v):
    return v

def low_keep(v):
    return (reduced_precision(v), None)

def low_pass(kept, grad):
    return (grad,)

def back_keep(v):
    return (v, None)

def back_low(kept, grad):
    return (reduced_precision(grad),)
reduced_precision.defvjp(low_keep, low_pass)
reduced_backward.defvjp(back_keep, back_low)

def leaky_smooth(value):
    return 0.2 * value + 0.8 * jax.nn.silu(value)

def shifted(values, offset):
    length = values.shape[-1]
    zeros = jnp.zeros(values.shape[:-1] + (abs(offset),), values.dtype)
    if offset > 0:
        return jnp.concatenate([values[..., offset:], zeros], axis=-1)
    return jnp.concatenate([zeros, values[..., :length + offset]], axis=-1)

def same_seg(segment_index, offset):
    tagged = segment_index + 1
    return (shifted(tagged, offset) == tagged).astype(jnp.float32)

def matrix_product(form, left, right):
    return jnp.einsum(form, left, right, precision=lax.Precision.HIGHEST)

def forward_pass(upsample_direction, upsample_gain, upsample_bias, dilated_direction, paired_direction, residual_gain, residual_bias, signal, segment_index):
    upsample_weight = reduced_precision(upsample_gain[:, None] * upsample_direction / jnp.sqrt(lax.optimization_barrier(jnp.sum(upsample_direction * upsample_direction, axis=1, keepdims=True))))
    dilated_kernel_weight = reduced_precision(residual_gain[:, 0, :, None] * dilated_direction / jnp.sqrt(lax.optimization_barrier(jnp.sum(dilated_direction * dilated_direction, axis=2, keepdims=True))))
    paired_kernel_weight = reduced_precision(residual_gain[:, 1:, :, None] * paired_direction / jnp.sqrt(lax.optimization_barrier(jnp.sum(paired_direction * paired_direction, axis=3, keepdims=True))))
    frames = signal.shape[-1]
    first = reduced_precision(leaky_smooth(signal))
    taps_out = matrix_product('ik,it->kt', upsample_weight, first).reshape(CHANNELS_OUT, KERNEL, frames)
    in_prev = same_seg(segment_index, -1)[None, :]
    in_next = same_seg(segment_index, 1)[None, :]
    even_out = taps_out[:, 1] + shifted(taps_out[:, 3], -1) * in_prev
    odd_out = taps_out[:, 2] + shifted(taps_out[:, 0], 1) * in_next
    hidden = jnp.stack([even_out, odd_out], axis=-1).reshape(CHANNELS_OUT, 2 * frames) + upsample_bias[:, None]
    hidden = reduced_backward(hidden)
    seg_out = jnp.repeat(segment_index, 2, axis=-1)
    for block_number in range(RESIDUAL_BLOCKS):
        dilation = 3 ** block_number
        minus = same_seg(seg_out, -dilation)[None, :]
        plus = same_seg(seg_out, dilation)[None, :]
        pre_conv = reduced_precision(leaky_smooth(hidden))
        hidden_low = reduced_precision(hidden)
        stacked_blocks = jnp.concatenate([shifted(pre_conv, -dilation) * minus, pre_conv, shifted(pre_conv, dilation) * plus], axis=0)
        dilated_output = reduced_backward(matrix_product('kv,vz->kz', dilated_kernel_weight[block_number], stacked_blocks) + residual_bias[block_number, 0][:, None])
        activated = reduced_precision(leaky_smooth(dilated_output))
        branch = matrix_product('oi,it->ot', paired_kernel_weight[block_number, 0], activated) + residual_bias[block_number, 1][:, None]
        shortcut = matrix_product('oi,it->ot', paired_kernel_weight[block_number, 1], hidden_low) + residual_bias[block_number, 2][:, None]
        hidden = reduced_backward(branch + shortcut)
    return hidden

def reference(signal, segments, cotangent, upsample_direction, upsample_gain, upsample_bias, dilated_direction, paired_direction, residual_gain, residual_bias):
    model_parameters = tuple((block_item.astype(jnp.float32) for block_item in (upsample_direction, upsample_gain, upsample_bias, dilated_direction, paired_direction, residual_gain, residual_bias)))

    def one_pack(carry, block_item):
        pack_signal, packed_segment, pack_cot = block_item

        def closed_form(upsample_direction_shard, upsample_gain_shard, upsample_bias_shard, dilated_direction_shard, paired_direction_shard, residual_gain_shard, residual_bias_shard, signal_single):
            return forward_pass(upsample_direction_shard, upsample_gain_shard, upsample_bias_shard, dilated_direction_shard, paired_direction_shard, residual_gain_shard, residual_bias_shard, signal_single, packed_segment)
        result, pull = jax.vjp(closed_form, *model_parameters, pack_signal.astype(jnp.float32))
        grads = pull(pack_cot.astype(jnp.float32))
        carry = tuple((total + grad for total, grad in zip(carry, grads[:7])))
        return (carry, (result.astype(jnp.bfloat16), grads[7].astype(jnp.bfloat16)))
    start = tuple((jnp.zeros_like(block_item) for block_item in model_parameters))
    totals, stacked_out = lax.scan(one_pack, start, (signal, segments, cotangent))
    return (stacked_out[0], stacked_out[1], totals[0], totals[1], totals[2], totals[3], totals[4], totals[5], totals[6])
```

```python
import functools
import jax, jax.numpy as jnp
from jax import lax
from jax.experimental import pallas as pl
from jax.experimental.pallas import tpu as pltpu

BF=jnp.bfloat16; F32=jnp.float32
RS=64
L=128

def dot(a,b):
    return jnp.dot(a,b,preferred_element_type=F32)
def dot_nt(a,b):
    return lax.dot_general(a,b,(((1,),(1,)),((),())),preferred_element_type=F32)

def act_pair(v):
    th=jnp.tanh(0.5*v); a=0.6+0.4*th
    return v*a, a+(0.2*v)*(1.0-th*th)

KINDS={-1:0,1:1,-2:2,2:3,-4:4,4:5,-5:6,5:7}

def main_kernel(NC, packs, cpp, *refs):
    ins=refs[:11]
    ws=ins[3:8]+(ins[8],ins[10])
    def body(masks,*sc):
        wsc=sc[:7]
        for a,b in zip(wsc,ws): a[...]=b[...]
        main_body(NC,packs,cpp,*ins[:3],*wsc[:6],ins[9],wsc[6],*refs[11:],masks,sc[7:])
    pl.run_scoped(body,pltpu.VMEM((packs*cpp,8,16,L),BF),*[pltpu.VMEM(w.shape,w.dtype) for w in ws],*[pltpu.VMEM((RS,64,L),BF)]*23)

def main_body(NC, packs, cpp, sig_h, seg, cot_h, wu, wv, wd, wdb, pf, pt, bias, perm,
                out_h, sg_h, dU, dD, dP, dB,
                sig, cot, outb, sgb, sem_in, sem_out, masks, rings):
    NCOL=packs*cpp
    (FIRST,DFIRST,PRE0,PRE1,PRE2,HID0,HID1,HID2,DH0,DH1,DH2,ACT0,ACT1,ACT2,DD0,DD1,G2,G1,G0,GD0,GD1,GD2,GU)=range(23)
    PRE=(PRE0,PRE1,PRE2);HID=(HID0,HID1,HID2);DH=(DH0,DH1,DH2);ACT=(ACT0,ACT1,ACT2);DD=(DD0,DD1);GD=(GD0,GD1,GD2);G=(G0,G1,G2)
    W=NC*L
    def copies_in(p):
        return (pltpu.make_async_copy(sig_h.at[p],sig.at[p],sem_in.at[0,p]),
                pltpu.make_async_copy(cot_h.at[p],cot.at[p],sem_in.at[1,p]))
    def copies_out(p):
        return (pltpu.make_async_copy(outb.at[p],out_h.at[p],sem_out.at[0,p]),
                pltpu.make_async_copy(sgb.at[p],sg_h.at[p],sem_out.at[1,p]))
    for p in range(packs):
        for c in copies_in(p): c.start()
    dU[...]=jnp.zeros_like(dU); dD[...]=jnp.zeros_like(dD); dP[...]=jnp.zeros_like(dP); dB[...]=jnp.zeros_like(dB)
    def zero(r,_):
        for q in rings: q[r]=jnp.zeros((64,L),BF)
        return 0
    lax.fori_loop(0,RS,zero,0)
    T=cpp*L
    for k,kind in KINDS.items():
        s=seg[...]
        pos=lax.broadcasted_iota(jnp.int32,s.shape,1)
        r=pltpu.roll(s,(-k)%T,1)
        ok=(r==s)&(pos+k>=0)&(pos+k<T)
        m=ok.astype(F32)
        for p in range(packs):
            mp=jnp.broadcast_to(m[p:p+1,:],(16,T)).astype(BF)
            for c in range(cpp):
                masks[p*cpp+c,kind]=mp[:,c*L:(c+1)*L]
    def slot(j): return j & (RS-1)
    def ld(r,j0,n=NC):
        return jnp.concatenate([rings[r][slot(j0+k)] for k in range(n)],axis=1) if n>1 else rings[r][slot(j0)]
    def st(r,j0,v):
        v=v.astype(BF)
        for k in range(NC): rings[r][slot(j0+k)]=v[:,k*L:(k+1)*L]
    def clampj(j): return jnp.clip(j,0,NCOL-1)
    def mask(kind,j0,rows):
        cols=[]
        for k in range(NC):
            m=masks[clampj(j0+k),KINDS[kind]]
            cols.append(jnp.concatenate([m]*(rows//16),axis=0))
        return jnp.concatenate(cols,axis=1)
    def shf(x,k):
        if k>0: return pltpu.roll(x[:,L:],W+L-k,1)[:,:W]
        return pltpu.roll(x[:,:W+L],-k,1)[:,L:]
    def stack(r,j0,b):
        x=ld(r,j0-1,NC+2)
        E=x[:32]; O=x[32:]
        a_=(3**b-1)//2; b_=(3**b+1)//2
        Em=x[:32,L:L+W]; Om=x[32:,L:L+W]
        Omin=shf(O,-b_)*mask(-b_,j0,32)
        Opl=shf(O,a_)*mask(a_,j0,32) if a_ else Om
        Emin=shf(E,-a_)*mask(-a_,j0,32) if a_ else Em
        Epl=shf(E,b_)*mask(b_,j0,32)
        return jnp.concatenate([Omin,Em,Opl],axis=0), jnp.concatenate([Emin,Om,Epl],axis=0)
    def per_phase(w,xE,xO): return jnp.concatenate([dot(w,xE),dot(w,xO)],axis=0)
    def rowsum(v):
        s=v[:32]+v[32:]
        r=s[:,:L]
        for k in range(1,NC): r=r+s[:,k*L:(k+1)*L]
        return r
    def bcol(i):
        x=bias[i]
        return jnp.concatenate([jnp.concatenate([x]*NC,axis=1)]*2,axis=0)
    D=NC+1
    d0=0; dl=[D*s for s in range(9)]
    def pc(j):
        jc=clampj(j)
        return jc//cpp, jc%cpp
    def po(j):
        ok=(j>=0)&(j<NCOL)
        jc=clampj(j)
        return jnp.where(ok,jc//cpp,packs), jc%cpp
    def st_V(base):
        j=base-dl[8]
        x=ld(GU,j-1,NC+2)
        gu=x[:,L:L+W]
        gt=jnp.concatenate([gu, shf(x[:32],1)*mask(1,j,32), shf(x[32:],-1)*mask(-1,j,32)],axis=0)
        fi=ld(FIRST,j); df=ld(DFIRST,j)
        y=dot(wv[...],gt)
        yield
        dU[...]+=dot_nt(gt,fi)
        yield
        sgv=(y*df.astype(F32)).astype(BF)
        for k in range(NC):
            p,c=po(j+k)
            sgb[p,:,pl.ds(pl.multiple_of(c*L,L),L)]=sgv[:,k*L:(k+1)*L]
    def st_B(base,b,si):
        j=base-dl[si]
        sE,sO=stack(GD[b],j,b)
        g=ld(G[b],j); pre=ld(PRE[b],j); dh=ld(DH[b],j); act=ld(ACT[b],j); hid=ld(HID[b],j)
        ddp=ld(DD[b-1],j) if b else None
        A=per_phase(wdb[b],sE,sO)
        S=per_phase(pt[b,1],g[:32],g[32:])
        yield
        dD[b]+=dot_nt(sE,pre[:32])+dot_nt(sO,pre[32:])
        yield
        gf=dh.astype(F32)*A+S
        gl=gf.astype(BF)
        if b==0:
            st(GU,j,gl); dB[0,2]+=rowsum(gf)
        else:
            st(G[b-1],j,gl)
            ag=per_phase(pt[b-1,0],gl[:32],gl[32:])
        yield
        dP[b]+=dot_nt(jnp.concatenate([act[:32],hid[:32]],axis=0),g[:32])+dot_nt(jnp.concatenate([act[32:],hid[32:]],axis=0),g[32:])
        if b:
            dB[b-1,1]+=rowsum(gf)
            yield
            gd=ddp.astype(F32)*ag
            dB[b-1,0]+=rowsum(gd)
            st(GD[b-1],j,gd)
    def st_D(base,b):
        j=base-dl[2+b]
        sE,sO=stack(PRE[b],j,b)
        hid=ld(HID[b],j)
        dil=per_phase(wd[b],sE,sO)
        if b==2:
            cs=[]
            for k in range(NC):
                p,c=pc(j+k)
                cs.append(cot[p,:,pl.ds(pl.multiple_of(c*2*L,2*L),2*L)])
            cz=dot(jnp.concatenate(cs,axis=0),perm[1])
        yield
        yield
        dil=dil+bcol(1+2*b)
        act,dd=act_pair(dil)
        act=act.astype(BF)
        st(ACT[b],j,act)
        h=per_phase(pf[b],jnp.concatenate([act[:32],hid[:32]],axis=0),jnp.concatenate([act[32:],hid[32:]],axis=0))
        if b<2:
            st(DD[b],j,dd)
        else:
            gE=jnp.concatenate([cz[k*32:(k+1)*32,:L] for k in range(NC)],axis=1)
            gO=jnp.concatenate([cz[k*32:(k+1)*32,L:] for k in range(NC)],axis=1)
            gf=jnp.concatenate([gE,gO],axis=0)
            vk=[jnp.where((j+k>=0)&(j+k<NCOL),1.0,0.0) for k in range(NC)]
            gf=jnp.concatenate([gf[:,k*L:(k+1)*L]*vk[k] for k in range(NC)],axis=1)
            gl=gf.astype(BF)
            st(G2,j,gl)
            dB[2,1]+=rowsum(gf)
            ag=per_phase(pt[2,0],gl[:32],gl[32:])
        yield
        yield
        h=h+bcol(2+2*b)
        if b<2:
            pre,dh=act_pair(h)
            st(PRE[b+1],j,pre); st(HID[b+1],j,h); st(DH[b+1],j,dh)
        else:
            ho=h.astype(BF)
            z=jnp.concatenate([jnp.concatenate([ho[:32,k*L:(k+1)*L],ho[32:,k*L:(k+1)*L]],axis=1) for k in range(NC)],axis=0)
            z=dot(z,perm[0])
            gd=dd*ag
            dB[2,0]+=rowsum(gd)
            st(GD2,j,gd)
            yield
            z=z.astype(BF)
            for k in range(NC):
                p,c=po(j+k)
                outb[p,:,pl.ds(pl.multiple_of(c*2*L,2*L),2*L)]=z[k*32:(k+1)*32]
    def st_U(base):
        j=base-dl[1]
        x=ld(FIRST,j-1,NC+2)
        f0=x[:,L:L+W]
        fm=shf(x,-1)*mask(-1,j,64); fp=shf(x,1)*mask(1,j,64)
        h=jnp.concatenate([dot(wu[0],jnp.concatenate([f0,fm],axis=0)),dot(wu[1],jnp.concatenate([f0,fp],axis=0))],axis=0)
        yield
        yield
        h=h+bcol(0)
        pre,dh=act_pair(h)
        st(PRE0,j,pre); st(HID0,j,h); st(DH0,j,dh)
    def st_F(base):
        j=base
        xs=[]
        for k in range(NC):
            p,c=pc(j+k)
            xs.append(sig[p,:,pl.ds(pl.multiple_of(c*L,L),L)])
        x=jnp.concatenate(xs,axis=1)
        yield
        fv,dv=act_pair(x.astype(F32))
        st(FIRST,j,fv); st(DFIRST,j,dv)
    def step(i,_):
        base=i*NC
        gens=[st_V(base),st_D(base,2),st_B(base,0,7),st_B(base,1,6),st_D(base,1),st_B(base,2,5),st_D(base,0),st_U(base),st_F(base)]
        while gens:
            nxt=[]
            for g in gens:
                try: next(g); nxt.append(g)
                except StopIteration: pass
            gens=nxt
        return 0
    ipp=cpp//NC
    def outer(g,_):
        for c in copies_in(g): c.wait()
        lax.fori_loop(g*ipp,(g+1)*ipp,step,0)
        @pl.when(g>=2)
        def _():
            for c in copies_out(g-2): c.start()
        return 0
    lax.fori_loop(0,packs,outer,0)
    tot=packs*ipp-(-dl[8]//NC)
    lax.fori_loop(packs*ipp,tot,step,0)
    for p in (packs-2,packs-1):
        for c in copies_out(p): c.start()
    for p in range(packs):
        for c in copies_out(p): c.wait()

def make_perm():
    r=jnp.arange(2*L)[:,None]; c=jnp.arange(2*L)[None,:]
    tgt=jnp.where(r<L,2*r,2*(r-L)+1)
    P=(tgt==c).astype(BF)
    return jnp.stack([P,P.T])

def prep(uw,dw,pw,ub,rb):
    taps=uw.reshape(64,32,4)
    t=[taps[:,:,k] for k in range(4)]
    wu=jnp.stack([jnp.concatenate([t[1].T,t[3].T],1),jnp.concatenate([t[2].T,t[0].T],1)])
    wv=jnp.concatenate([t[1],t[2],t[3],t[0]],1)
    d3=dw.reshape(3,32,3,32)
    wdb=jnp.concatenate([d3[:,:,2].transpose(0,2,1),d3[:,:,1].transpose(0,2,1),d3[:,:,0].transpose(0,2,1)],2)
    pf=jnp.concatenate([pw[:,0],pw[:,1]],2)
    pt=pw.transpose(0,1,3,2)
    ub=ub.astype(F32); rb=rb.astype(F32)
    bl=[ub]
    for b in range(3): bl+= [rb[b,0], rb[b,1]+rb[b,2]]
    bias=jnp.broadcast_to(jnp.stack(bl)[:,:,None],(7,32,L))
    return wu,wv,dw,wdb,pf,pt,bias

def main_call(NC,signal,segments,cot,wts):
    packs,cin,T=signal.shape
    cpp=T//L
    wu,wv,wd,wdb,pf,pt,bias=wts
    perm=make_perm()
    V=pl.BlockSpec(memory_space=pltpu.VMEM); A=pl.BlockSpec(memory_space=pl.ANY)
    return pl.pallas_call(
        functools.partial(main_kernel,NC,packs,cpp),
        name="section",
        out_shape=(jax.ShapeDtypeStruct(cot.shape,BF),jax.ShapeDtypeStruct(signal.shape,BF),
            jax.ShapeDtypeStruct((128,64),F32),jax.ShapeDtypeStruct((3,96,32),F32),jax.ShapeDtypeStruct((3,64,32),F32),jax.ShapeDtypeStruct((3,3,32,L),F32)),
        in_specs=[A,V,A]+[V]*8, out_specs=(A,A,V,V,V,V),
        scratch_shapes=[pltpu.VMEM(signal.shape,BF),pltpu.VMEM(cot.shape,BF),
            pltpu.VMEM((packs+1,32,2*T),BF),pltpu.VMEM((packs+1,64,T),BF),
            pltpu.SemaphoreType.DMA((2,packs)),pltpu.SemaphoreType.DMA((2,packs))],
        compiler_params=pltpu.CompilerParams(vmem_limit_bytes=63<<20),
    )(signal,segments,cot,wu,wv,wd,wdb,pf,pt,bias,perm)

from jax.sharding import PartitionSpec as P


def pack_local(ud, ug, ub, dd, pd, rg, rb):
    return jnp.concatenate([v.reshape(-1) for v in (ud, dd, pd, ug, ub, rg, rb)])


def norm_backward(direction, scale, norm, weight_grad):
    inner = jnp.sum(weight_grad * direction, axis=-1, keepdims=True)
    scale_grad = (inner / norm)[..., 0]
    return scale / norm * (weight_grad - inner / (norm * norm) * direction), scale_grad


def per_device(nd, nf, signal, segments, cotangent, ud, ug, ub, dd, pd, rg, rb):
    shards = (ud, dd, pd, ug, ub, rg, rb)
    flat = pack_local(ud, ug, ub, dd, pd, rg, rb)
    full = lax.all_gather(flat, ("dp", "fsdp"), axis=0, tiled=False).reshape(nd, nf, -1)
    sizes = [v.size for v in shards]
    parts, at = [], 0
    for v, n in zip(shards, sizes):
        parts.append(full[:, :, at:at + n].reshape((nd, nf) + v.shape))
        at += n
    ud_f = parts[0].transpose(0, 2, 1, 3).reshape(64, 128).astype(F32)
    dd_f = parts[1].transpose(2, 0, 3, 1, 4).reshape(3, 32, 96).astype(F32)
    pd_f = parts[2].transpose(2, 3, 0, 4, 1, 5).reshape(3, 2, 32, 32).astype(F32)
    ug_f = parts[3][0].reshape(64).astype(F32)
    ub_f = parts[4][0].reshape(32)
    rg_f = parts[5][0].transpose(1, 2, 0, 3).reshape(3, 3, 32).astype(F32)
    rb_f = parts[6][0].transpose(1, 2, 0, 3).reshape(3, 3, 32)
    un = jnp.sqrt(jnp.sum(ud_f * ud_f, axis=1, keepdims=True))
    dn = jnp.sqrt(jnp.sum(dd_f * dd_f, axis=2, keepdims=True))
    pn = jnp.sqrt(jnp.sum(pd_f * pd_f, axis=3, keepdims=True))
    us, ds, ps = ug_f[:, None], rg_f[:, 0, :, None], rg_f[:, 1:, :, None]
    wts = prep((us * ud_f / un).astype(BF), (ds * dd_f / dn).astype(BF), (ps * pd_f / pn).astype(BF), ub_f, rb_f)
    out, sg, gu, gd, gp, gb = main_call(NC, signal, segments, cotangent, wts)
    gu = gu.reshape(4, 32, 64)[jnp.array([3, 0, 1, 2])].transpose(2, 1, 0).reshape(64, 128)
    gd = gd.reshape(3, 3, 32, 32)[:, ::-1].transpose(0, 2, 1, 3).reshape(3, 32, 96)
    gp = gp.reshape(3, 2, 32, 32).transpose(0, 1, 3, 2)
    gb = gb.sum(-1)
    gud, gug = norm_backward(ud_f, us, un, gu)
    gdd, gdg = norm_backward(dd_f, ds, dn, gd)
    gpd, gpg = norm_backward(pd_f, ps, pn, gp)
    grg = jnp.concatenate([gdg[:, None], gpg], axis=1)
    grb = jnp.stack([gb[:, 0], gb[:, 1], gb[:, 1]], axis=1)
    a, b = ud.shape
    m0 = gud.reshape(nd, a, nf, b).transpose(0, 2, 1, 3).reshape(nd, nf, -1)
    a, b = dd.shape[1:]
    m1 = gdd.reshape(3, nd, a, nf, b).transpose(1, 3, 0, 2, 4).reshape(nd, nf, -1)
    a, b = pd.shape[2:]
    m2 = gpd.reshape(3, 2, nd, a, nf, b).transpose(2, 4, 0, 1, 3, 5).reshape(nd, nf, -1)
    sm = [gug.reshape(nf, -1), gb[0, 2].reshape(nf, -1), grg.reshape(9, nf, -1).transpose(1, 0, 2).reshape(nf, -1),
          grb.reshape(9, nf, -1).transpose(1, 0, 2).reshape(nf, -1)]
    sm = jnp.broadcast_to(jnp.concatenate(sm, axis=1)[None], (nd, nf, sum(v.shape[1] for v in sm)))
    msg = jnp.concatenate([m0, m1, m2, sm], axis=2).reshape(nd * nf, -1)
    tot = lax.psum_scatter(msg, ("dp", "fsdp"), scatter_dimension=0, tiled=True)[0]
    res, at = [], 0
    for v, n in zip(shards, sizes):
        res.append(tot[at:at + n].reshape(v.shape))
        at += n
    return out, sg, res[0], res[3], res[4], res[1], res[2], res[5], res[6]


NC = 4


def solution(mesh):
    nd, nf = mesh.shape["dp"], mesh.shape["fsdp"]
    return jax.shard_map(
        functools.partial(per_device, nd, nf),
        mesh=mesh,
        in_specs=(
            P(("dp", "fsdp"), None, None),
            P(("dp", "fsdp"), None),
            P(("dp", "fsdp"), None, None),
            P("dp", "fsdp"),
            P("fsdp"),
            P("fsdp"),
            P(None, "dp", "fsdp"),
            P(None, None, "dp", "fsdp"),
            P(None, None, "fsdp"),
            P(None, None, "fsdp"),
        ),
        out_specs=(
            P(("dp", "fsdp"), None, None),
            P(("dp", "fsdp"), None, None),
            P("dp", "fsdp"),
            P("fsdp"),
            P("fsdp"),
            P(None, "dp", "fsdp"),
            P(None, None, "dp", "fsdp"),
            P(None, None, "fsdp"),
            P(None, None, "fsdp"),
        ),
        check_vma=False,
    )
```

```python
import functools
import jax, jax.numpy as jnp
from jax import lax
from jax.experimental import pallas as pl
from jax.experimental.pallas import tpu as pltpu

BF=jnp.bfloat16; F32=jnp.float32
RS=64
L=128

def dot(a,b):
    return jnp.dot(a,b,preferred_element_type=F32)
def dot_nt(a,b):
    return lax.dot_general(a,b,(((1,),(1,)),((),())),preferred_element_type=F32)

def act_pair(v):
    th=jnp.tanh(0.5*v); a=0.6+0.4*th
    return v*a, a+(0.2*v)*(1.0-th*th)

KINDS={-1:0,1:1,-2:2,2:3,-4:4,4:5,-5:6,5:7}

class Lay:
    def __init__(self, nd, nf):
        self.nd, self.nf, self.n = nd, nf, nd * nf
        self.wu, self.wd, self.wp, self.wr, self.wg = 128 // nf, 96 // nf, 32 // nf, 32 // nf, 64 // nf
        self.pu = 64 // nd // 8
        at = 0
        self.u = []
        for _ in range(self.pu):
            self.u.append(at)
            at += self.wu
        self.d = []
        for _ in range(3):
            self.d.append(at)
            at += self.wd
        self.p = []
        for _ in range(6):
            self.p.append(at)
            at += self.wp
        self.r = []
        for _ in range(3):
            self.r.append(at)
            at += self.wr
        self.g = at
        assert at + self.wg <= 128


def lane8(): return lax.broadcasted_iota(jnp.int32,(8,L),1)


def move(x, frm, to):
    k=(to-frm)%L
    return x if k==0 else pltpu.roll(x,k,1)


def put(acc, x, frm, to, w):
    lane=lane8()
    return jnp.where((lane>=to)&(lane<to+w),move(x,frm,to),acc)


def tap_perm():
    r=lax.broadcasted_iota(jnp.int32,(L,L),0); c=lax.broadcasted_iota(jnp.int32,(L,L),1)
    pos=((r&3)+3)&3
    return (c==pos*32+(r>>2)).astype(F32).astype(BF)


def square(x):
    return jnp.concatenate([x,jnp.zeros((L-x.shape[0],L),F32)],axis=0) if x.shape[0]<L else x


def prologue(lay, recv, wu, wv, wd, wdb, pf, pt, bias, dirs, cols):
    nd,nf=lay.nd,lay.nf
    z=jnp.zeros((8,L),F32)
    def gather(i, o, w, off=0, acc=None):
        acc=z if acc is None else acc
        for f in range(nf):
            acc=put(acc,recv[i*nf+f].astype(F32),o,off+f*w,w)
        return acc
    ud=jnp.concatenate([gather(i,o,lay.wu) for i in range(nd) for o in lay.u],axis=0)
    dd=[jnp.concatenate([gather(i,lay.d[b],lay.wd) for i in range(nd)],axis=0) for b in range(3)]
    pd=[jnp.concatenate([gather(i,lay.p[2*b+1],lay.wp,32,gather(i,lay.p[2*b],lay.wp)) for i in range(nd)],axis=0) for b in range(3)]
    sm=[gather(0,lay.r[b],lay.wr) for b in range(3)]+[gather(0,lay.g,lay.wg),gather(0,lay.g,lay.wr)]
    st=square(jnp.concatenate(sm,axis=0)).T
    def col(q,rows): return jnp.broadcast_to(st[:rows,q:q+1],(rows,L))
    def norm(x): return jnp.broadcast_to(jnp.sqrt(jnp.sum(x*x,axis=1,keepdims=True)),x.shape)
    n=norm(ud); g=col(24,64)
    dirs[0:64]=ud; cols[0,0:64]=g/n; cols[1,0:64]=1.0/n
    w=dot((g*ud/n).astype(BF),tap_perm())
    wv[...]=w.astype(BF)
    m=jnp.concatenate([w,pltpu.roll(w,64,1)],axis=0).T
    wu[0]=m[:32].astype(BF); wu[1]=m[32:64].astype(BF)
    bias[0]=col(33,32)
    lane=lax.broadcasted_iota(jnp.int32,(32,L),1)
    for b in range(3):
        r=64+32*b
        x=dd[b]; n=norm(x); g=col(8*b,32)
        dirs[r:r+32]=x; cols[0,r:r+32]=g/n; cols[1,r:r+32]=1.0/n
        w=(g*x/n).astype(BF)
        wd[b]=w[:,:96]
        w=w.astype(F32)
        m=square(jnp.concatenate([pltpu.roll(w,64,1),pltpu.roll(w,96,1),w],axis=0)).T
        wdb[b]=m[:32,:96].astype(BF)
        r=160+32*b
        x=pd[b]
        n=jnp.where(lane<32,norm(jnp.where(lane<32,x,0.0)),norm(jnp.where(lane<32,0.0,x)))
        g=jnp.where(lane<32,col(8*b+1,32),col(8*b+2,32))
        dirs[r:r+32]=x; cols[0,r:r+32]=g/n; cols[1,r:r+32]=1.0/n
        w=(g*x/n).astype(BF)
        pf[b]=w[:,:64]
        m=square(w.astype(F32)).T
        pt[b]=m[:64,:32].astype(BF)
        bias[1+2*b]=col(8*b+3,32)
        bias[2+2*b]=col(8*b+4,32)+col(8*b+5,32)


def epilogue(lay, dU, dD, dP, dB, dirs, cols, tmp, msgs):
    nd,nf=lay.nd,lay.nf
    def rs(x): return jnp.sum(x,axis=1,keepdims=True)
    lane=lax.broadcasted_iota(jnp.int32,(64,L),1); lane32=lane[:32]
    C=jnp.zeros((64,L),F32)
    def place(C,q,c):
        c=jnp.broadcast_to(c,(c.shape[0],L))
        if c.shape[0]==32: c=jnp.concatenate([c,jnp.zeros((32,L),F32)],axis=0)
        return jnp.where(lane==q,c,C)
    perm=tap_perm()
    v=dot(dirs[0:64].astype(BF),perm); w=dU[...]; s=cols[0,0:64]; i=cols[1,0:64]
    inner=rs(w*v)
    C=place(C,24,inner*i)
    g=s*(w-(inner*i*i)*v)
    gu=dot_nt(g.astype(BF),perm)
    gd=[];gp=[]
    tmp[...]=jnp.zeros_like(tmp)
    for b in range(3):
        r=64+32*b
        for t in range(3): tmp[b,:,t*32:t*32+32]=dD[b,(2-t)*32:(3-t)*32]
        v=dirs[r:r+32]; w=tmp[b]; s=cols[0,r:r+32]; i=cols[1,r:r+32]
        inner=rs(w*v)
        C=place(C,8*b,inner*i)
        gd.append(s*(w-(inner*i*i)*v))
        r=160+32*b
        tmp[3+b,:,:64]=dP[b]
        v=dirs[r:r+32]; w=tmp[3+b]; s=cols[0,r:r+32]; i=cols[1,r:r+32]
        p=w*v
        inner=jnp.where(lane32<32,rs(jnp.where(lane32<32,p,0.0)),rs(jnp.where(lane32<32,0.0,p)))
        C=place(C,8*b+1,inner[:,:1]*i[:,:1])
        C=place(C,8*b+2,inner[:,32:33]*i[:,32:33])
        gp.append(s*(w-(inner*i*i)*v))
        C=place(C,8*b+3,rs(dB[b,0]))
        o=rs(dB[b,1])
        C=place(C,8*b+4,o); C=place(C,8*b+5,o)
    C=place(C,33,rs(dB[0,2]))
    S=square(C).T
    for f in range(nf):
        sm=jnp.zeros((8,L),F32)
        for b in range(3): sm=put(sm,S[8*b:8*b+8],f*lay.wr,lay.r[b],lay.wr)
        sm=put(sm,S[24:32],f*lay.wg,lay.g,lay.wg)
        row=lax.broadcasted_iota(jnp.int32,(8,L),0)
        sm=jnp.where(row==1,put(sm,S[32:40],f*lay.wr,lay.g,lay.wr),sm)
        for d in range(nd):
            x=sm
            for p in range(lay.pu): x=put(x,gu[(d*lay.pu+p)*8:(d*lay.pu+p)*8+8],f*lay.wu,lay.u[p],lay.wu)
            for b in range(3):
                x=put(x,gd[b][8*d:8*d+8],f*lay.wd,lay.d[b],lay.wd)
                for j in range(2): x=put(x,gp[b][8*d:8*d+8],32*j+f*lay.wp,lay.p[2*b+j],lay.wp)
            msgs[d*nf+f]=x.astype(BF)


def main_kernel(NC, packs, cpp, lay, sig_h, seg, cot_h, recv, perm_in, out_h, sg_h, msgs,
                sig, cot, outb, sgb, dU, dD, dP, dB, dirs, cols, tmp, bias, sem_in, sem_out):
    def body(masks, wu, wv, wd, wdb, pf, pt, perm, *rings):
        perm[...]=perm_in[...]
        main_body(NC,packs,cpp,lay,recv,sig_h,seg,cot_h,wu,wv,wd,wdb,pf,pt,bias,perm,out_h,sg_h,msgs,dU,dD,dP,dB,
                  sig,cot,outb,sgb,dirs,cols,tmp,sem_in,sem_out,masks,rings)
    pl.run_scoped(body,pltpu.VMEM((packs*cpp,8,16,L),BF),
                  pltpu.VMEM((2,32,L),BF),pltpu.VMEM((64,L),BF),pltpu.VMEM((3,32,96),BF),pltpu.VMEM((3,32,96),BF),
                  pltpu.VMEM((3,32,64),BF),pltpu.VMEM((3,64,32),BF),pltpu.VMEM((2,2*L,2*L),BF),
                  *[pltpu.VMEM((RS,64,L),BF)]*23)


def main_body(NC, packs, cpp, lay, recv, sig_h, seg, cot_h, wu, wv, wd, wdb, pf, pt, bias, perm,
              out_h, sg_h, msgs, dU, dD, dP, dB, sig, cot, outb, sgb, dirs, cols, tmp, sem_in, sem_out, masks, rings):
    NCOL=packs*cpp
    (FIRST,DFIRST,PRE0,PRE1,PRE2,HID0,HID1,HID2,DH0,DH1,DH2,ACT0,ACT1,ACT2,DD0,DD1,G2,G1,G0,GD0,GD1,GD2,GU)=range(23)
    PRE=(PRE0,PRE1,PRE2);HID=(HID0,HID1,HID2);DH=(DH0,DH1,DH2);ACT=(ACT0,ACT1,ACT2);DD=(DD0,DD1);GD=(GD0,GD1,GD2);G=(G0,G1,G2)
    W=NC*L
    def copies_in(p):
        return (pltpu.make_async_copy(sig_h.at[p],sig.at[p],sem_in.at[0,p]),
                pltpu.make_async_copy(cot_h.at[p],cot.at[p],sem_in.at[1,p]))
    def copies_out(p):
        return (pltpu.make_async_copy(outb.at[p],out_h.at[p],sem_out.at[0,p]),
                pltpu.make_async_copy(sgb.at[p],sg_h.at[p],sem_out.at[1,p]))
    for p in range(packs):
        for c in copies_in(p): c.start()
    prologue(lay,recv,wu,wv,wd,wdb,pf,pt,bias,dirs,cols)
    dU[...]=jnp.zeros_like(dU); dD[...]=jnp.zeros_like(dD); dP[...]=jnp.zeros_like(dP); dB[...]=jnp.zeros_like(dB)
    def zero(r,_):
        for q in rings: q[r]=jnp.zeros((64,L),BF)
        return 0
    lax.fori_loop(0,RS,zero,0)
    T=cpp*L
    for k,kind in KINDS.items():
        s=seg[...]
        pos=lax.broadcasted_iota(jnp.int32,s.shape,1)
        r=pltpu.roll(s,(-k)%T,1)
        ok=(r==s)&(pos+k>=0)&(pos+k<T)
        m=ok.astype(F32)
        for p in range(packs):
            mp=jnp.broadcast_to(m[p:p+1,:],(16,T)).astype(BF)
            for c in range(cpp):
                masks[p*cpp+c,kind]=mp[:,c*L:(c+1)*L]
    def slot(j): return j & (RS-1)
    def ld(r,j0,n=NC):
        return jnp.concatenate([rings[r][slot(j0+k)] for k in range(n)],axis=1) if n>1 else rings[r][slot(j0)]
    def st(r,j0,v):
        v=v.astype(BF)
        for k in range(NC): rings[r][slot(j0+k)]=v[:,k*L:(k+1)*L]
    def clampj(j): return jnp.clip(j,0,NCOL-1)
    def mask(kind,j0,rows):
        cols=[]
        for k in range(NC):
            m=masks[clampj(j0+k),KINDS[kind]]
            cols.append(jnp.concatenate([m]*(rows//16),axis=0))
        return jnp.concatenate(cols,axis=1)
    def shf(x,k):
        if k>0: return pltpu.roll(x[:,L:],W+L-k,1)[:,:W]
        return pltpu.roll(x[:,:W+L],-k,1)[:,L:]
    def stack(r,j0,b):
        x=ld(r,j0-1,NC+2)
        E=x[:32]; O=x[32:]
        a_=(3**b-1)//2; b_=(3**b+1)//2
        Em=x[:32,L:L+W]; Om=x[32:,L:L+W]
        Omin=shf(O,-b_)*mask(-b_,j0,32)
        Opl=shf(O,a_)*mask(a_,j0,32) if a_ else Om
        Emin=shf(E,-a_)*mask(-a_,j0,32) if a_ else Em
        Epl=shf(E,b_)*mask(b_,j0,32)
        return jnp.concatenate([Omin,Em,Opl],axis=0), jnp.concatenate([Emin,Om,Epl],axis=0)
    def per_phase(w,xE,xO): return jnp.concatenate([dot(w,xE),dot(w,xO)],axis=0)
    def rowsum(v):
        s=v[:32]+v[32:]
        r=s[:,:L]
        for k in range(1,NC): r=r+s[:,k*L:(k+1)*L]
        return r
    def bcol(i):
        x=bias[i]
        return jnp.concatenate([jnp.concatenate([x]*NC,axis=1)]*2,axis=0)
    D=NC+1
    d0=0; dl=[D*s for s in range(9)]
    def pc(j):
        jc=clampj(j)
        return jc//cpp, jc%cpp
    def po(j):
        ok=(j>=0)&(j<NCOL)
        jc=clampj(j)
        return jnp.where(ok,jc//cpp,packs), jc%cpp
    def st_V(base):
        j=base-dl[8]
        x=ld(GU,j-1,NC+2)
        gu=x[:,L:L+W]
        gt=jnp.concatenate([gu, shf(x[:32],1)*mask(1,j,32), shf(x[32:],-1)*mask(-1,j,32)],axis=0)
        fi=ld(FIRST,j); df=ld(DFIRST,j)
        y=dot(wv[...],gt)
        yield
        dU[...]+=dot_nt(fi,gt)
        yield
        sgv=(y*df.astype(F32)).astype(BF)
        for k in range(NC):
            p,c=po(j+k)
            sgb[p,:,pl.ds(pl.multiple_of(c*L,L),L)]=sgv[:,k*L:(k+1)*L]
    def st_B(base,b,si):
        j=base-dl[si]
        sE,sO=stack(GD[b],j,b)
        g=ld(G[b],j); pre=ld(PRE[b],j); dh=ld(DH[b],j); act=ld(ACT[b],j); hid=ld(HID[b],j)
        ddp=ld(DD[b-1],j) if b else None
        A=per_phase(wdb[b],sE,sO)
        S=per_phase(pt[b,32:],g[:32],g[32:])
        yield
        dD[b]+=dot_nt(sE,pre[:32])+dot_nt(sO,pre[32:])
        yield
        gf=dh.astype(F32)*A+S
        gl=gf.astype(BF)
        if b==0:
            st(GU,j,gl); dB[0,2]+=rowsum(gf)
        else:
            st(G[b-1],j,gl)
            ag=per_phase(pt[b-1,:32],gl[:32],gl[32:])
        yield
        dP[b]+=dot_nt(g[:32],jnp.concatenate([act[:32],hid[:32]],axis=0))+dot_nt(g[32:],jnp.concatenate([act[32:],hid[32:]],axis=0))
        if b:
            dB[b-1,1]+=rowsum(gf)
            yield
            gd=ddp.astype(F32)*ag
            dB[b-1,0]+=rowsum(gd)
            st(GD[b-1],j,gd)
    def st_D(base,b):
        j=base-dl[2+b]
        sE,sO=stack(PRE[b],j,b)
        hid=ld(HID[b],j)
        dil=per_phase(wd[b],sE,sO)
        if b==2:
            cs=[]
            for k in range(NC):
                p,c=pc(j+k)
                cs.append(cot[p,:,pl.ds(pl.multiple_of(c*2*L,2*L),2*L)])
            cz=dot(jnp.concatenate(cs,axis=0),perm[1])
        yield
        yield
        dil=dil+bcol(1+2*b)
        act,dd=act_pair(dil)
        act=act.astype(BF)
        st(ACT[b],j,act)
        h=per_phase(pf[b],jnp.concatenate([act[:32],hid[:32]],axis=0),jnp.concatenate([act[32:],hid[32:]],axis=0))
        if b<2:
            st(DD[b],j,dd)
        else:
            gE=jnp.concatenate([cz[k*32:(k+1)*32,:L] for k in range(NC)],axis=1)
            gO=jnp.concatenate([cz[k*32:(k+1)*32,L:] for k in range(NC)],axis=1)
            gf=jnp.concatenate([gE,gO],axis=0)
            vk=[jnp.where((j+k>=0)&(j+k<NCOL),1.0,0.0) for k in range(NC)]
            gf=jnp.concatenate([gf[:,k*L:(k+1)*L]*vk[k] for k in range(NC)],axis=1)
            gl=gf.astype(BF)
            st(G2,j,gl)
            dB[2,1]+=rowsum(gf)
            ag=per_phase(pt[2,:32],gl[:32],gl[32:])
        yield
        yield
        h=h+bcol(2+2*b)
        if b<2:
            pre,dh=act_pair(h)
            st(PRE[b+1],j,pre); st(HID[b+1],j,h); st(DH[b+1],j,dh)
        else:
            ho=h.astype(BF)
            z=jnp.concatenate([jnp.concatenate([ho[:32,k*L:(k+1)*L],ho[32:,k*L:(k+1)*L]],axis=1) for k in range(NC)],axis=0)
            z=dot(z,perm[0])
            gd=dd*ag
            dB[2,0]+=rowsum(gd)
            st(GD2,j,gd)
            yield
            z=z.astype(BF)
            for k in range(NC):
                p,c=po(j+k)
                outb[p,:,pl.ds(pl.multiple_of(c*2*L,2*L),2*L)]=z[k*32:(k+1)*32]
    def st_U(base):
        j=base-dl[1]
        x=ld(FIRST,j-1,NC+2)
        f0=x[:,L:L+W]
        fm=shf(x,-1)*mask(-1,j,64); fp=shf(x,1)*mask(1,j,64)
        h=jnp.concatenate([dot(wu[0],jnp.concatenate([f0,fm],axis=0)),dot(wu[1],jnp.concatenate([f0,fp],axis=0))],axis=0)
        yield
        yield
        h=h+bcol(0)
        pre,dh=act_pair(h)
        st(PRE0,j,pre); st(HID0,j,h); st(DH0,j,dh)
    def st_F(base):
        j=base
        xs=[]
        for k in range(NC):
            p,c=pc(j+k)
            xs.append(sig[p,:,pl.ds(pl.multiple_of(c*L,L),L)])
        x=jnp.concatenate(xs,axis=1)
        yield
        fv,dv=act_pair(x.astype(F32))
        st(FIRST,j,fv); st(DFIRST,j,dv)
    def step(i,_):
        base=i*NC
        gens=[st_V(base),st_D(base,2),st_B(base,0,7),st_B(base,1,6),st_D(base,1),st_B(base,2,5),st_D(base,0),st_U(base),st_F(base)]
        while gens:
            nxt=[]
            for g in gens:
                try: next(g); nxt.append(g)
                except StopIteration: pass
            gens=nxt
        return 0
    ipp=cpp//NC
    def outer(g,_):
        for c in copies_in(g): c.wait()
        lax.fori_loop(g*ipp,(g+1)*ipp,step,0)
        @pl.when(g>=2)
        def _():
            for c in copies_out(g-2): c.start()
        return 0
    lax.fori_loop(0,packs,outer,0)
    tot=packs*ipp-(-dl[8]//NC)
    lax.fori_loop(packs*ipp,tot,step,0)
    for p in (packs-2,packs-1):
        for c in copies_out(p): c.start()
    epilogue(lay,dU,dD,dP,dB,dirs,cols,tmp,msgs)
    for p in range(packs):
        for c in copies_out(p): c.wait()

def make_perm():
    r=jnp.arange(2*L)[:,None]; c=jnp.arange(2*L)[None,:]
    tgt=jnp.where(r<L,2*r,2*(r-L)+1)
    P=(tgt==c).astype(BF)
    return jnp.stack([P,P.T])


def main_call(NC, lay, signal, segments, cot, recv):
    packs,cin,T=signal.shape
    cpp=T//L
    V=pl.BlockSpec(memory_space=pltpu.VMEM); A=pl.BlockSpec(memory_space=pl.ANY)
    return pl.pallas_call(
        functools.partial(main_kernel,NC,packs,cpp,lay),
        name="section",
        out_shape=(jax.ShapeDtypeStruct(cot.shape,BF),jax.ShapeDtypeStruct(signal.shape,BF),jax.ShapeDtypeStruct((lay.n,8,L),BF)),
        in_specs=[A,V,A,V,V], out_specs=(A,A,V),
        scratch_shapes=[pltpu.VMEM(signal.shape,BF),pltpu.VMEM(cot.shape,BF),
            pltpu.VMEM((packs+1,32,2*T),BF),pltpu.VMEM((packs+1,64,T),BF),
            pltpu.VMEM((64,L),F32),pltpu.VMEM((3,96,32),F32),pltpu.VMEM((3,32,64),F32),pltpu.VMEM((3,3,32,L),F32),
            pltpu.VMEM((256,L),F32),pltpu.VMEM((2,256,L),F32),pltpu.VMEM((6,32,L),F32),pltpu.VMEM((7,32,L),F32),
            pltpu.SemaphoreType.DMA((2,packs)),pltpu.SemaphoreType.DMA((2,packs))],
        compiler_params=pltpu.CompilerParams(vmem_limit_bytes=63<<20),
    )(signal,segments,cot,recv,make_perm())

from jax.sharding import PartitionSpec as P

MESH = pl.DeviceIdType.MESH


def peer(lay, k):
    me = lax.axis_index("dp") * lay.nf + lax.axis_index("fsdp")
    t = lax.rem(me + k, lay.n)
    return me, t, {"dp": t // lay.nf, "fsdp": lax.rem(t, lay.nf)}


def greet(lay):
    barrier = pltpu.get_barrier_semaphore()

    def hello(k, c):
        _, _, dev = peer(lay, k)
        pl.semaphore_signal(barrier, inc=1, device_id=dev, device_id_type=MESH)
        return c

    lax.fori_loop(1, lay.n, hello, 0)
    return barrier


def exchange(lay, source, recv, send_sem, recv_sem):
    def copy(k):
        me, t, dev = peer(lay, k)
        return pltpu.make_async_remote_copy(
            src_ref=source(t), dst_ref=recv.at[me], send_sem=send_sem.at[k], recv_sem=recv_sem.at[k],
            device_id=dev, device_id_type=MESH)

    def start(k, c):
        copy(k).start()
        return c

    def finish(k, c):
        copy(k).wait()
        return c

    lax.fori_loop(1, lay.n, start, 0)
    lax.fori_loop(1, lay.n, finish, 0)


def gather_kernel(lay, ud, dd, pd, ug, ub, rg, rb, out, acc, msg, recv, send_sem, recv_sem):
    barrier = greet(lay)
    acc[...] = jnp.zeros_like(acc)
    for p, o in enumerate(lay.u):
        acc[:, o:o + lay.wu] = ud[8 * p:8 * p + 8].astype(F32)
    for b in range(3):
        acc[:, lay.d[b]:lay.d[b] + lay.wd] = dd[b].astype(F32)
        for j in range(2):
            o = lay.p[2 * b + j]
            acc[:, o:o + lay.wp] = pd[b, j].astype(F32)
        o = lay.r[b]
        acc[0:3, o:o + lay.wr] = rg[b].astype(F32)
        acc[3:6, o:o + lay.wr] = rb[b].astype(F32)
    acc[0:1, lay.g:lay.g + lay.wg] = ug[...].astype(F32)
    acc[1:2, lay.g:lay.g + lay.wr] = ub[...].astype(F32)
    msg[...] = acc[...].astype(BF)
    me = peer(lay, 0)[0]
    recv[me] = acc[...].astype(BF)
    pl.semaphore_wait(barrier, lay.n - 1)
    exchange(lay, lambda t: msg, recv, send_sem, recv_sem)
    out[...] = recv[...]


def scatter_kernel(lay, msgs, out, recv, send_sem, recv_sem):
    barrier = greet(lay)
    me = peer(lay, 0)[0]
    recv[me] = msgs[me]
    pl.semaphore_wait(barrier, lay.n - 1)
    exchange(lay, lambda t: msgs.at[t], recv, send_sem, recv_sem)
    out[...] = recv[...]


def sum_kernel(lay, recv, gud, gug, gub, gdd, gpd, grg, grb):
    t = recv[0].astype(F32)
    for s in range(1, lay.n):
        t = t + recv[s].astype(F32)
    for p, o in enumerate(lay.u):
        gud[8 * p:8 * p + 8] = t[:, o:o + lay.wu]
    for b in range(3):
        gdd[b] = t[:, lay.d[b]:lay.d[b] + lay.wd]
        for j in range(2):
            o = lay.p[2 * b + j]
            gpd[b, j] = t[:, o:o + lay.wp]
        o = lay.r[b]
        grg[b] = t[0:3, o:o + lay.wr]
        grb[b] = t[3:6, o:o + lay.wr]
    gug[...] = t[0:1, lay.g:lay.g + lay.wg]
    gub[...] = t[1:2, lay.g:lay.g + lay.wr]


def per_device(lay, signal, segments, cotangent, ud, ug, ub, dd, pd, rg, rb):
    V = pl.BlockSpec(memory_space=pltpu.VMEM)
    tiles = jax.ShapeDtypeStruct((lay.n, 8, L), BF)
    sems = [pltpu.SemaphoreType.DMA((lay.n,)), pltpu.SemaphoreType.DMA((lay.n,))]
    table = pl.pallas_call(
        functools.partial(gather_kernel, lay), name="gather_params", out_shape=tiles,
        in_specs=[V] * 7, out_specs=V,
        scratch_shapes=[pltpu.VMEM((8, L), F32), pltpu.VMEM((8, L), BF), pltpu.VMEM((lay.n, 8, L), BF)] + sems,
        compiler_params=pltpu.CompilerParams(collective_id=0, has_side_effects=True),
    )(ud, dd, pd, ug.reshape(1, -1), ub.reshape(1, -1), rg, rb)
    out, sg, msgs = main_call(NC, lay, signal, segments, cotangent, table)
    got = pl.pallas_call(
        functools.partial(scatter_kernel, lay), name="scatter_grads", out_shape=tiles,
        in_specs=[V], out_specs=V,
        scratch_shapes=[pltpu.VMEM((lay.n, 8, L), BF)] + sems,
        compiler_params=pltpu.CompilerParams(collective_id=1, has_side_effects=True),
    )(msgs)
    f = lambda *s: jax.ShapeDtypeStruct(s, F32)
    gud, gug, gub, gdd, gpd, grg, grb = pl.pallas_call(
        functools.partial(sum_kernel, lay), name="sum_grads",
        out_shape=(f(*ud.shape), f(1, ug.shape[0]), f(1, ub.shape[0]), f(*dd.shape), f(*pd.shape), f(*rg.shape), f(*rb.shape)),
        in_specs=[V], out_specs=(V,) * 7,
    )(got)
    return out, sg, gud, gug.reshape(-1), gub.reshape(-1), gdd, gpd, grg, grb


NC = 4


def solution(mesh):
    lay = Lay(mesh.shape["dp"], mesh.shape["fsdp"])
    return jax.shard_map(
        functools.partial(per_device, lay),
        mesh=mesh,
        in_specs=(
            P(("dp", "fsdp"), None, None),
            P(("dp", "fsdp"), None),
            P(("dp", "fsdp"), None, None),
            P("dp", "fsdp"),
            P("fsdp"),
            P("fsdp"),
            P(None, "dp", "fsdp"),
            P(None, None, "dp", "fsdp"),
            P(None, None, "fsdp"),
            P(None, None, "fsdp"),
        ),
        out_specs=(
            P(("dp", "fsdp"), None, None),
            P(("dp", "fsdp"), None, None),
            P("dp", "fsdp"),
            P("fsdp"),
            P("fsdp"),
            P(None, "dp", "fsdp"),
            P(None, None, "dp", "fsdp"),
            P(None, None, "fsdp"),
            P(None, None, "fsdp"),
        ),
        check_vma=False,
    )
```

```python
import functools
import jax, jax.numpy as jnp
from jax import lax
from jax.experimental import pallas as pl
from jax.experimental.pallas import tpu as pltpu

BF=jnp.bfloat16; F32=jnp.float32
RS=64
L=128

def dot(a,b):
    return jnp.dot(a,b,preferred_element_type=F32)
def dot_nt(a,b):
    return lax.dot_general(a,b,(((1,),(1,)),((),())),preferred_element_type=F32)

def act_pair(h):
    h=h.astype(F32)
    v=h.astype(BF); w=(0.2*h).astype(BF)
    c=lambda x: jnp.asarray(x,BF)
    th=jnp.tanh(c(0.5)*v); t=c(3.0)+c(2.0)*th; q=c(1.0)-th*th
    return w*t, t+v*q

KINDS={-1:0,1:1,-2:2,2:3,-4:4,4:5,-5:6,5:7}

NAMES=("V1","S","NTP","A","B2","B3","cz","D1","D2","G2f","D3","GD2f","O","U1","U2","F")


def FULL(e):
    V1,S,NTP,A,B2,B3,cz,D1,D2,G2f,D3,GD2f,O,U1,U2,F=[e[k] for k in NAMES]
    cz(); NTP(0); S(0); S(1); S(2); NTP(1)
    D1(2); V1(); A(0); A(1); D1(1)
    D2(2); G2f(); A(2); B2(0); B2(1)
    D1(0); D3(2); GD2f(); B2(2); B3(1); D2(1)
    U1(); O(); B3(2); D3(1); D2(0); U2(); F()
    NTP(2); D3(0)


def FILL(e):
    V1,S,NTP,A,B2,B3,cz,D1,D2,G2f,D3,GD2f,O,U1,U2,F=[e[k] for k in NAMES]
    D1(1); D1(0); U1(); D2(1); D2(0); U2(); F(); D3(1); D3(0)


def DRAIN(e):
    V1,S,NTP,A,B2,B3,cz,D1,D2,G2f,D3,GD2f,O,U1,U2,F=[e[k] for k in NAMES]
    NTP(0); S(0); S(1); S(2)
    V1(); A(0); A(1); A(2); B2(0); B2(1); B2(2); NTP(1); NTP(2); B3(1); B3(2)


class Lay:
    def __init__(self, nd, nf):
        self.nd, self.nf, self.n = nd, nf, nd * nf
        self.wu, self.wd, self.wp, self.wr, self.wg = 128 // nf, 96 // nf, 32 // nf, 32 // nf, 64 // nf
        self.pu = 64 // nd // 8
        at = 0
        self.u = []
        for _ in range(self.pu):
            self.u.append(at)
            at += self.wu
        self.d = []
        for _ in range(3):
            self.d.append(at)
            at += self.wd
        self.p = []
        for _ in range(6):
            self.p.append(at)
            at += self.wp
        self.r = []
        for _ in range(3):
            self.r.append(at)
            at += self.wr
        self.g = at
        assert at + self.wg <= 128


def lane8(): return lax.broadcasted_iota(jnp.int32,(8,L),1)


def move(x, frm, to):
    k=(to-frm)%L
    return x if k==0 else pltpu.roll(x,k,1)


def put(acc, x, frm, to, w):
    lane=lane8()
    return jnp.where((lane>=to)&(lane<to+w),move(x,frm,to),acc)


def tap_perm():
    r=lax.broadcasted_iota(jnp.int32,(L,L),0); c=lax.broadcasted_iota(jnp.int32,(L,L),1)
    pos=((r&3)+3)&3
    return (c==pos*32+(r>>2)).astype(F32).astype(BF)


def square(x):
    return jnp.concatenate([x,jnp.zeros((L-x.shape[0],L),F32)],axis=0) if x.shape[0]<L else x


def prologue(lay, recv, wu, wv, wd, wdb, pf, pt, bias, dirs, cols):
    nd,nf=lay.nd,lay.nf
    z=jnp.zeros((8,L),F32)
    def gather(i, o, w, off=0, acc=None):
        acc=z if acc is None else acc
        for f in range(nf):
            acc=put(acc,recv[i*nf+f].astype(F32),o,off+f*w,w)
        return acc
    ud=jnp.concatenate([gather(i,o,lay.wu) for i in range(nd) for o in lay.u],axis=0)
    dd=[jnp.concatenate([gather(i,lay.d[b],lay.wd) for i in range(nd)],axis=0) for b in range(3)]
    pd=[jnp.concatenate([gather(i,lay.p[2*b+1],lay.wp,32,gather(i,lay.p[2*b],lay.wp)) for i in range(nd)],axis=0) for b in range(3)]
    sm=[gather(0,lay.r[b],lay.wr) for b in range(3)]+[gather(0,lay.g,lay.wg),gather(0,lay.g,lay.wr)]
    st=square(jnp.concatenate(sm,axis=0)).T
    def col(q,rows): return jnp.broadcast_to(st[:rows,q:q+1],(rows,L))
    def norm(x): return jnp.broadcast_to(jnp.sqrt(jnp.sum(x*x,axis=1,keepdims=True)),x.shape)
    n=norm(ud); g=col(24,64)
    dirs[0:64]=ud; cols[0,0:64]=g/n; cols[1,0:64]=1.0/n
    w=dot((g*ud/n).astype(BF),tap_perm())
    wv[...]=w.astype(BF)
    m=jnp.concatenate([w,pltpu.roll(w,64,1)],axis=0).T
    wu[0]=m[:32].astype(BF); wu[1]=m[32:64].astype(BF)
    bias[0]=col(33,32)
    lane=lax.broadcasted_iota(jnp.int32,(32,L),1)
    for b in range(3):
        r=64+32*b
        x=dd[b]; n=norm(x); g=col(8*b,32)
        dirs[r:r+32]=x; cols[0,r:r+32]=g/n; cols[1,r:r+32]=1.0/n
        w=(g*x/n).astype(BF)
        wd[b]=w[:,:96]
        w=w.astype(F32)
        m=square(jnp.concatenate([pltpu.roll(w,64,1),pltpu.roll(w,96,1),w],axis=0)).T
        wdb[b]=m[:32,:96].astype(BF)
        r=160+32*b
        x=pd[b]
        n=jnp.where(lane<32,norm(jnp.where(lane<32,x,0.0)),norm(jnp.where(lane<32,0.0,x)))
        g=jnp.where(lane<32,col(8*b+1,32),col(8*b+2,32))
        dirs[r:r+32]=x; cols[0,r:r+32]=g/n; cols[1,r:r+32]=1.0/n
        w=(g*x/n).astype(BF)
        pf[b]=w[:,:64]
        m=square(w.astype(F32)).T
        pt[b]=m[:64,:32].astype(BF)
        bias[1+2*b]=col(8*b+3,32)
        bias[2+2*b]=col(8*b+4,32)+col(8*b+5,32)


def epilogue(lay, dU, dD, dP, dB, dirs, cols, tmp, msgs):
    nd,nf=lay.nd,lay.nf
    def rs(x): return jnp.sum(x,axis=1,keepdims=True)
    lane=lax.broadcasted_iota(jnp.int32,(64,L),1); lane32=lane[:32]
    C=jnp.zeros((64,L),F32)
    def place(C,q,c):
        c=jnp.broadcast_to(c,(c.shape[0],L))
        if c.shape[0]==32: c=jnp.concatenate([c,jnp.zeros((32,L),F32)],axis=0)
        return jnp.where(lane==q,c,C)
    perm=tap_perm()
    v=dot(dirs[0:64].astype(BF),perm); w=dU[...].T[:64]; s=cols[0,0:64]; i=cols[1,0:64]
    inner=rs(w*v)
    C=place(C,24,inner*i)
    g=s*(w-(inner*i*i)*v)
    gu=dot_nt(g.astype(BF),perm)
    gd=[];gp=[]
    tmp[...]=jnp.zeros_like(tmp)
    for b in range(3):
        r=64+32*b
        for t in range(3): tmp[b,:,t*32:t*32+32]=dD[b,(2-t)*32:(3-t)*32]
        v=dirs[r:r+32]; w=tmp[b]; s=cols[0,r:r+32]; i=cols[1,r:r+32]
        inner=rs(w*v)
        C=place(C,8*b,inner*i)
        gd.append(s*(w-(inner*i*i)*v))
        r=160+32*b
        m=jnp.concatenate([dP[b],jnp.zeros((64,L),F32)],axis=0).T
        tmp[3+b]=m[:32]
        v=dirs[r:r+32]; w=tmp[3+b]; s=cols[0,r:r+32]; i=cols[1,r:r+32]
        p=w*v
        inner=jnp.where(lane32<32,rs(jnp.where(lane32<32,p,0.0)),rs(jnp.where(lane32<32,0.0,p)))
        C=place(C,8*b+1,inner[:,:1]*i[:,:1])
        C=place(C,8*b+2,inner[:,32:33]*i[:,32:33])
        gp.append(s*(w-(inner*i*i)*v))
        C=place(C,8*b+3,rs(dB[b,0]))
        o=rs(dB[b,1])
        C=place(C,8*b+4,o); C=place(C,8*b+5,o)
    C=place(C,33,rs(dB[0,2]))
    S=square(C).T
    for f in range(nf):
        sm=jnp.zeros((8,L),F32)
        for b in range(3): sm=put(sm,S[8*b:8*b+8],f*lay.wr,lay.r[b],lay.wr)
        sm=put(sm,S[24:32],f*lay.wg,lay.g,lay.wg)
        row=lax.broadcasted_iota(jnp.int32,(8,L),0)
        sm=jnp.where(row==1,put(sm,S[32:40],f*lay.wr,lay.g,lay.wr),sm)
        for d in range(nd):
            x=sm
            for p in range(lay.pu): x=put(x,gu[(d*lay.pu+p)*8:(d*lay.pu+p)*8+8],f*lay.wu,lay.u[p],lay.wu)
            for b in range(3):
                x=put(x,gd[b][8*d:8*d+8],f*lay.wd,lay.d[b],lay.wd)
                for j in range(2): x=put(x,gp[b][8*d:8*d+8],32*j+f*lay.wp,lay.p[2*b+j],lay.wp)
            msgs[d*nf+f]=x.astype(BF)


def main_kernel(NC, packs, cpp, lay, sig_h, seg, cot_h, recv, out_h, sg_h, msgs,
                sig, cot, outb, sgb, dU, dD, dP, dB, dirs, cols, tmp, bias, sem_in, sem_out):
    def body(masks, wu, wv, wd, wdb, pf, pt, perm, *rings):
        make_perm(perm)
        main_body(NC,packs,cpp,lay,recv,sig_h,seg,cot_h,wu,wv,wd,wdb,pf,pt,bias,perm,out_h,sg_h,msgs,dU,dD,dP,dB,
                  sig,cot,outb,sgb,dirs,cols,tmp,sem_in,sem_out,masks,rings)
    pl.run_scoped(body,pltpu.VMEM((packs*cpp,8,16,L),BF),
                  pltpu.VMEM((2,32,L),BF),pltpu.VMEM((64,L),BF),pltpu.VMEM((3,32,96),BF),pltpu.VMEM((3,32,96),BF),
                  pltpu.VMEM((3,32,64),BF),pltpu.VMEM((3,64,32),BF),pltpu.VMEM((2,2*L,2*L),BF),
                  *[pltpu.VMEM((RS,64,L),BF)]*23)


def main_body(NC, packs, cpp, lay, recv, sig_h, seg, cot_h, wu, wv, wd, wdb, pf, pt, bias, perm,
              out_h, sg_h, msgs, dU, dD, dP, dB, sig, cot, outb, sgb, dirs, cols, tmp, sem_in, sem_out, masks, rings):
    NCOL=packs*cpp
    (FIRST,DFIRST,PRE0,PRE1,PRE2,HID0,HID1,HID2,DH0,DH1,DH2,ACT0,ACT1,ACT2,DD0,DD1,G2,G1,G0,GD0,GD1,GD2,GU)=range(23)
    PRE=(PRE0,PRE1,PRE2);HID=(HID0,HID1,HID2);DH=(DH0,DH1,DH2);ACT=(ACT0,ACT1,ACT2);DD=(DD0,DD1);GD=(GD0,GD1,GD2);G=(G0,G1,G2)
    W=NC*L
    def copies_in(p):
        return (pltpu.make_async_copy(sig_h.at[p],sig.at[p],sem_in.at[0,p]),
                pltpu.make_async_copy(cot_h.at[p],cot.at[p],sem_in.at[1,p]))
    def copies_out(p):
        return (pltpu.make_async_copy(outb.at[p],out_h.at[p],sem_out.at[0,p]),
                pltpu.make_async_copy(sgb.at[p],sg_h.at[p],sem_out.at[1,p]))
    for p in range(packs):
        for c in copies_in(p): c.start()
    prologue(lay,recv,wu,wv,wd,wdb,pf,pt,bias,dirs,cols)
    dU[...]=jnp.zeros_like(dU); dD[...]=jnp.zeros_like(dD); dP[...]=jnp.zeros_like(dP); dB[...]=jnp.zeros_like(dB)
    def zero(r,_):
        for q in rings: q[r]=jnp.zeros((64,L),BF)
        return 0
    lax.fori_loop(0,RS,zero,0)
    T=cpp*L
    for k,kind in KINDS.items():
        s=seg[...]
        pos=lax.broadcasted_iota(jnp.int32,s.shape,1)
        r=pltpu.roll(s,(-k)%T,1)
        ok=(r==s)&(pos+k>=0)&(pos+k<T)
        m=ok.astype(F32)
        for p in range(packs):
            mp=jnp.broadcast_to(m[p:p+1,:],(16,T)).astype(BF)
            for c in range(cpp):
                masks[p*cpp+c,kind]=mp[:,c*L:(c+1)*L]
    def slot(j): return j & (RS-1)
    def ld(r,j0,n=NC):
        return jnp.concatenate([rings[r][slot(j0+k)] for k in range(n)],axis=1) if n>1 else rings[r][slot(j0)]
    def st(r,j0,v):
        v=v.astype(BF)
        for k in range(NC): rings[r][slot(j0+k)]=v[:,k*L:(k+1)*L]
    def clampj(j): return jnp.clip(j,0,NCOL-1)
    def mask(kind,j0,rows):
        cols=[]
        for k in range(NC):
            m=masks[clampj(j0+k),KINDS[kind]]
            cols.append(jnp.concatenate([m]*(rows//16),axis=0))
        return jnp.concatenate(cols,axis=1)
    def shf(x,k):
        if k>0: return pltpu.roll(x[:,L:],W+L-k,1)[:,:W]
        return pltpu.roll(x[:,:W+L],-k,1)[:,L:]
    def stack(r,j0,b):
        x=ld(r,j0-1,NC+2)
        E=x[:32]; O=x[32:]
        a_=(3**b-1)//2; b_=(3**b+1)//2
        Em=x[:32,L:L+W]; Om=x[32:,L:L+W]
        Omin=shf(O,-b_)*mask(-b_,j0,32)
        Opl=shf(O,a_)*mask(a_,j0,32) if a_ else Om
        Emin=shf(E,-a_)*mask(-a_,j0,32) if a_ else Em
        Epl=shf(E,b_)*mask(b_,j0,32)
        return jnp.concatenate([Omin,Em,Opl],axis=0), jnp.concatenate([Emin,Om,Epl],axis=0)
    def per_phase(w,xE,xO): return jnp.concatenate([dot(w,xE),dot(w,xO)],axis=0)
    def rowsum(v):
        s=v[:32]+v[32:]
        r=s[:,:L]
        for k in range(1,NC): r=r+s[:,k*L:(k+1)*L]
        return r
    def bcol(i):
        x=bias[i]
        return jnp.concatenate([jnp.concatenate([x]*NC,axis=1)]*2,axis=0)
    D=NC+1
    d0=0; dl=[D*s for s in range(9)]
    def pc(j):
        jc=clampj(j)
        return jc//cpp, jc%cpp
    def po(j):
        ok=(j>=0)&(j<NCOL)
        jc=clampj(j)
        return jnp.where(ok,jc//cpp,packs), jc%cpp
    def cat0(*v): return jnp.concatenate(v,axis=0)
    def step(order,i,_):
        base=i*NC
        X={}
        jv=base-dl[8]; jb=[base-dl[7],base-dl[6],base-dl[5]]; jd=[base-dl[2],base-dl[3],base-dl[4]]; ju=base-dl[1]
        def V1():
            x=ld(GU,jv-1,NC+2)
            gu=x[:,L:L+W]
            gt=cat0(gu, shf(x[:32],1)*mask(1,jv,32), shf(x[32:],-1)*mask(-1,jv,32))
            y=dot(wv[...],gt)
            dU[:,:64]+=dot_nt(gt,ld(FIRST,jv))
            sgv=((0.2*y)*ld(DFIRST,jv).astype(F32)).astype(BF)
            for k in range(NC):
                p,c=po(jv+k)
                sgb[p,:,pl.ds(pl.multiple_of(c*L,L),L)]=sgv[:,k*L:(k+1)*L]
        def S(b):
            g=ld(G[b],jb[b])
            X['S',b]=per_phase(pt[b,32:],g[:32],g[32:])
        def NTP(b):
            g=ld(G[b],jb[b]); act=ld(ACT[b],jb[b]); hid=ld(HID[b],jb[b])
            dP[b,:,:32]+=dot_nt(cat0(act[:32],hid[:32]),g[:32])+dot_nt(cat0(act[32:],hid[32:]),g[32:])
        def A(b):
            sE,sO=stack(GD[b],jb[b],b)
            X['A',b]=per_phase(wdb[b],sE,sO)
            pre=ld(PRE[b],jb[b])
            dD[b]+=dot_nt(sE,pre[:32])+dot_nt(sO,pre[32:])
        def B2(b):
            gf=ld(DH[b],jb[b]).astype(F32)*(0.2*X['A',b])+X['S',b]
            gl=gf.astype(BF)
            if b==0:
                st(GU,jb[b],gl); dB[0,2]+=rowsum(gf)
            else:
                st(G[b-1],jb[b],gl); dB[b-1,1]+=rowsum(gf)
                X['ag',b-1]=per_phase(pt[b-1,:32],gl[:32],gl[32:])
        def B3(b):
            gd=ld(DD[b-1],jb[b]).astype(F32)*(0.2*X['ag',b-1])
            dB[b-1,0]+=rowsum(gd)
            st(GD[b-1],jb[b],gd)
        def cz():
            cs=[]
            for k in range(NC):
                p,c=pc(jd[2]+k)
                cs.append(cot[p,:,pl.ds(pl.multiple_of(c*2*L,2*L),2*L)])
            X['cz']=dot(cat0(*cs),perm[1])
        def D1(b):
            sE,sO=stack(PRE[b],jd[b],b)
            X['dil',b]=per_phase(wd[b],sE,sO)
        def D2(b):
            act,dd=act_pair(X['dil',b]+bcol(1+2*b))
            act=act.astype(BF)
            st(ACT[b],jd[b],act)
            if b<2: st(DD[b],jd[b],dd)
            else: X['dd']=dd
            hid=ld(HID[b],jd[b])
            X['h',b]=per_phase(pf[b],cat0(act[:32],hid[:32]),cat0(act[32:],hid[32:]))
        def G2f():
            cz=X['cz']; j=jd[2]
            gE=jnp.concatenate([cz[k*32:(k+1)*32,:L] for k in range(NC)],axis=1)
            gO=jnp.concatenate([cz[k*32:(k+1)*32,L:] for k in range(NC)],axis=1)
            gf=cat0(gE,gO)
            vk=[jnp.where((j+k>=0)&(j+k<NCOL),1.0,0.0) for k in range(NC)]
            gf=jnp.concatenate([gf[:,k*L:(k+1)*L]*vk[k] for k in range(NC)],axis=1)
            gl=gf.astype(BF)
            st(G2,j,gl)
            dB[2,1]+=rowsum(gf)
            X['ag',2]=per_phase(pt[2,:32],gl[:32],gl[32:])
        def D3(b):
            h=X['h',b]+bcol(2+2*b)
            if b<2:
                pre,dh=act_pair(h)
                st(PRE[b+1],jd[b],pre); st(HID[b+1],jd[b],h); st(DH[b+1],jd[b],dh)
            else:
                ho=h.astype(BF)
                z=cat0(*[jnp.concatenate([ho[:32,k*L:(k+1)*L],ho[32:,k*L:(k+1)*L]],axis=1) for k in range(NC)])
                X['z']=dot(z,perm[0])
        def GD2f():
            gd=X['dd'].astype(F32)*(0.2*X['ag',2])
            dB[2,0]+=rowsum(gd)
            st(GD2,jd[2],gd)
        def O():
            z=X['z'].astype(BF)
            for k in range(NC):
                p,c=po(jd[2]+k)
                outb[p,:,pl.ds(pl.multiple_of(c*2*L,2*L),2*L)]=z[k*32:(k+1)*32]
        def U1():
            x=ld(FIRST,ju-1,NC+2)
            f0=x[:,L:L+W]
            fm=shf(x,-1)*mask(-1,ju,64); fp=shf(x,1)*mask(1,ju,64)
            X['u']=cat0(dot(wu[0],cat0(f0,fm)),dot(wu[1],cat0(f0,fp)))
        def U2():
            h=X['u']+bcol(0)
            pre,dh=act_pair(h)
            st(PRE0,ju,pre); st(HID0,ju,h); st(DH0,ju,dh)
        def F():
            xs=[]
            for k in range(NC):
                p,c=pc(base+k)
                xs.append(sig[p,:,pl.ds(pl.multiple_of(c*L,L),L)])
            fv,dv=act_pair(jnp.concatenate(xs,axis=1))
            st(FIRST,base,fv); st(DFIRST,base,dv)
        order(dict(locals()))
        return 0
    lo=lambda d: -((NC-1-d)//NC)
    hi=lambda d: (NCOL-1+d)//NC+1
    first_full=lo(dl[4]); last_full=hi(dl[4]); total=hi(dl[8])
    ipp=cpp//NC
    done=(cpp-1+dl[8])//NC+1
    for c in copies_in(0): c.wait()
    lax.fori_loop(0,first_full,functools.partial(step,FILL),0)
    def full(i,c):
        @pl.when((lax.rem(i,ipp)==0)&(i<packs*ipp))
        def _():
            for q in copies_in(lax.div(i,ipp)): q.wait()
        @pl.when((lax.rem(i,ipp)==done%ipp)&(i>=done))
        def _():
            for q in copies_out(lax.div(i-done,ipp)): q.start()
        return step(FULL,i,c)
    lax.fori_loop(first_full,last_full,full,0)
    started=[p for p in range(packs) if p*ipp+done<last_full]
    for k in range(NC*(total-last_full)+2):
        for r in (G2,GD2): rings[r][slot(NCOL+k)]=jnp.zeros((64,L),BF)
    lax.fori_loop(last_full,total,functools.partial(step,DRAIN),0)
    for p in range(len(started),packs):
        for c in copies_out(p): c.start()
    epilogue(lay,dU,dD,dP,dB,dirs,cols,tmp,msgs)
    for p in range(packs):
        for c in copies_out(p): c.wait()


def make_perm(perm):
    r=lax.broadcasted_iota(jnp.int32,(2*L,2*L),0); c=lax.broadcasted_iota(jnp.int32,(2*L,2*L),1)
    to=lambda x: jnp.where(x<L,2*x,2*(x-L)+1)
    perm[0]=(to(r)==c).astype(F32).astype(BF)
    perm[1]=(to(c)==r).astype(F32).astype(BF)


def main_call(NC, lay, signal, segments, cot, recv):
    packs,cin,T=signal.shape
    cpp=T//L
    V=pl.BlockSpec(memory_space=pltpu.VMEM); A=pl.BlockSpec(memory_space=pl.ANY)
    return pl.pallas_call(
        functools.partial(main_kernel,NC,packs,cpp,lay),
        name="section",
        out_shape=(jax.ShapeDtypeStruct(cot.shape,BF),jax.ShapeDtypeStruct(signal.shape,BF),jax.ShapeDtypeStruct((lay.n,8,L),BF)),
        in_specs=[A,V,A,V], out_specs=(A,A,V),
        scratch_shapes=[pltpu.VMEM(signal.shape,BF),pltpu.VMEM(cot.shape,BF),
            pltpu.VMEM((packs+1,32,2*T),BF),pltpu.VMEM((packs+1,64,T),BF),
            pltpu.VMEM((L,L),F32),pltpu.VMEM((3,96,32),F32),pltpu.VMEM((3,64,L),F32),pltpu.VMEM((3,3,32,L),F32),
            pltpu.VMEM((256,L),F32),pltpu.VMEM((2,256,L),F32),pltpu.VMEM((6,32,L),F32),pltpu.VMEM((7,32,L),F32),
            pltpu.SemaphoreType.DMA((2,packs)),pltpu.SemaphoreType.DMA((2,packs))],
        compiler_params=pltpu.CompilerParams(vmem_limit_bytes=54<<20),
    )(signal,segments,cot,recv)

from jax.sharding import PartitionSpec as P

MESH = pl.DeviceIdType.MESH


def peer(lay, k):
    me = lax.axis_index("dp") * lay.nf + lax.axis_index("fsdp")
    t = lax.rem(me + k, lay.n)
    return me, t, {"dp": t // lay.nf, "fsdp": lax.rem(t, lay.nf)}


def greet(lay):
    barrier = pltpu.get_barrier_semaphore()

    def hello(k, c):
        _, _, dev = peer(lay, k)
        pl.semaphore_signal(barrier, inc=1, device_id=dev, device_id_type=MESH)
        return c

    lax.fori_loop(1, lay.n, hello, 0)
    return barrier


def exchange(lay, source, recv, send_sem, recv_sem):
    def copy(k):
        me, t, dev = peer(lay, k)
        return pltpu.make_async_remote_copy(
            src_ref=source(t), dst_ref=recv.at[me], send_sem=send_sem.at[k], recv_sem=recv_sem.at[k],
            device_id=dev, device_id_type=MESH)

    def start(k, c):
        copy(k).start()
        return c

    def finish(k, c):
        copy(k).wait()
        return c

    lax.fori_loop(1, lay.n, start, 0)
    lax.fori_loop(1, lay.n, finish, 0)


def gather_kernel(lay, ud, dd, pd, ug, ub, rg, rb, out, acc, sq, msg, recv, send_sem, recv_sem):
    barrier = greet(lay)
    acc[...] = jnp.zeros_like(acc)
    sq[...] = jnp.zeros_like(sq)
    for p, o in enumerate(lay.u):
        acc[:, o:o + lay.wu] = ud[8 * p:8 * p + 8].astype(F32)
    for b in range(3):
        acc[:, lay.d[b]:lay.d[b] + lay.wd] = dd[b].astype(F32)
        for j in range(2):
            o = (2 * b + j) * lay.wp
            sq[o:o + lay.wp, 0:8] = pd[b, j].astype(F32)
        o = lay.r[b]
        acc[0:3, o:o + lay.wr] = rg[b].astype(F32)
        acc[3:6, o:o + lay.wr] = rb[b].astype(F32)
    acc[0:1, lay.g:lay.g + lay.wg] = ug[...].astype(F32)
    acc[1:2, lay.g:lay.g + lay.wr] = ub[...].astype(F32)
    full = put(acc[...], sq[...].T[:8], 0, lay.p[0], 6 * lay.wp).astype(BF)
    msg[...] = full
    me = peer(lay, 0)[0]
    recv[me] = full
    pl.semaphore_wait(barrier, lay.n - 1)
    exchange(lay, lambda t: msg, recv, send_sem, recv_sem)
    out[...] = recv[...]


def scatter_kernel(lay, msgs, out, recv, send_sem, recv_sem):
    barrier = greet(lay)
    me = peer(lay, 0)[0]
    recv[me] = msgs[me]
    pl.semaphore_wait(barrier, lay.n - 1)
    exchange(lay, lambda t: msgs.at[t], recv, send_sem, recv_sem)
    out[...] = recv[...]


def sum_kernel(lay, recv, gud, gug, gub, gdd, gpd, grg, grb):
    t = recv[0].astype(F32)
    for s in range(1, lay.n):
        t = t + recv[s].astype(F32)
    m = jnp.concatenate([move(t, lay.p[0], 0), jnp.zeros((L - 8, L), F32)], axis=0).T
    for p, o in enumerate(lay.u):
        gud[8 * p:8 * p + 8] = t[:, o:o + lay.wu]
    for b in range(3):
        gdd[b] = t[:, lay.d[b]:lay.d[b] + lay.wd]
        for j in range(2):
            o = (2 * b + j) * lay.wp
            gpd[b, j] = m[o:o + lay.wp, 0:8]
        o = lay.r[b]
        grg[b] = t[0:3, o:o + lay.wr]
        grb[b] = t[3:6, o:o + lay.wr]
    gug[...] = t[0:1, lay.g:lay.g + lay.wg]
    gub[...] = t[1:2, lay.g:lay.g + lay.wr]


def per_device(lay, signal, segments, cotangent, ud, ug, ub, dd, pd, rg, rb):
    V = pl.BlockSpec(memory_space=pltpu.VMEM)
    tiles = jax.ShapeDtypeStruct((lay.n, 8, L), BF)
    sems = [pltpu.SemaphoreType.DMA((lay.n,)), pltpu.SemaphoreType.DMA((lay.n,))]
    table = pl.pallas_call(
        functools.partial(gather_kernel, lay), name="gather_params", out_shape=tiles,
        in_specs=[V] * 7, out_specs=V,
        scratch_shapes=[pltpu.VMEM((8, L), F32), pltpu.VMEM((L, L), F32), pltpu.VMEM((8, L), BF), pltpu.VMEM((lay.n, 8, L), BF)] + sems,
        compiler_params=pltpu.CompilerParams(collective_id=0, has_side_effects=True),
    )(ud, dd, pd.transpose(0, 1, 3, 2), ug.reshape(1, -1), ub.reshape(1, -1), rg, rb)
    out, sg, msgs = main_call(NC, lay, signal, segments, cotangent, table)
    got = pl.pallas_call(
        functools.partial(scatter_kernel, lay), name="scatter_grads", out_shape=tiles,
        in_specs=[V], out_specs=V,
        scratch_shapes=[pltpu.VMEM((lay.n, 8, L), BF)] + sems,
        compiler_params=pltpu.CompilerParams(collective_id=1, has_side_effects=True),
    )(msgs)
    f = lambda *s: jax.ShapeDtypeStruct(s, F32)
    gud, gug, gub, gdd, gpd, grg, grb = pl.pallas_call(
        functools.partial(sum_kernel, lay), name="sum_grads",
        out_shape=(f(*ud.shape), f(1, ug.shape[0]), f(1, ub.shape[0]), f(*dd.shape), f(3, 2, pd.shape[3], pd.shape[2]), f(*rg.shape), f(*rb.shape)),
        in_specs=[V], out_specs=(V,) * 7,
    )(got)
    return out, sg, gud, gug.reshape(-1), gub.reshape(-1), gdd, gpd.transpose(0, 1, 3, 2), grg, grb


NC = 4


def solution(mesh):
    lay = Lay(mesh.shape["dp"], mesh.shape["fsdp"])
    return jax.shard_map(
        functools.partial(per_device, lay),
        mesh=mesh,
        in_specs=(
            P(("dp", "fsdp"), None, None),
            P(("dp", "fsdp"), None),
            P(("dp", "fsdp"), None, None),
            P("dp", "fsdp"),
            P("fsdp"),
            P("fsdp"),
            P(None, "dp", "fsdp"),
            P(None, None, "dp", "fsdp"),
            P(None, None, "fsdp"),
            P(None, None, "fsdp"),
        ),
        out_specs=(
            P(("dp", "fsdp"), None, None),
            P(("dp", "fsdp"), None, None),
            P("dp", "fsdp"),
            P("fsdp"),
            P("fsdp"),
            P(None, "dp", "fsdp"),
            P(None, None, "dp", "fsdp"),
            P(None, None, "fsdp"),
            P(None, None, "fsdp"),
        ),
        check_vma=False,
    )
```

```python
import functools
import jax, jax.numpy as jnp
from jax import lax
from jax.experimental import pallas as pl
from jax.experimental.pallas import tpu as pltpu

BF=jnp.bfloat16; F32=jnp.float32
L=128

def dot(a,b):
    return jnp.dot(a,b,preferred_element_type=F32)
def dot_nt(a,b):
    return lax.dot_general(a,b,(((1,),(1,)),((),())),preferred_element_type=F32)

def act_pair(h):
    h=h.astype(F32)
    v=h.astype(BF); w=(0.2*h).astype(BF)
    c=lambda x: jnp.asarray(x,BF)
    th=jnp.tanh(c(0.5)*v); t=c(3.0)+c(2.0)*th; q=c(1.0)-th*th
    return w*t, t+v*q

KINDS={-1:0,1:1,-2:2,2:3,-4:4,4:5,-5:6,5:7}

NAMES=("V1","NT","A","B2","AG","PW","PA","B3","D1","D2","G2f","D3","GD2f","O","U1","U2","F")


def FULL(e):
    V1,NT,A,B2,AG,PW,PA,B3,D1,D2,G2f,D3,GD2f,O,U1,U2,F=[e[k] for k in NAMES]
    NT(2); NT(1); D1(2); A(2); G2f(); D1(1); D2(2); PA(2)
    D2(1); B2(2); A(0); A(1); D3(2); D1(0); V1(); PA(1)
    O(); D3(1); B2(1); B2(0); B3(2); NT(0); D2(0); PA(0)
    U1(); GD2f(); U2(); B3(1); D3(0); F()


def lags(NC):
    out=[0]
    for k in range(8):
        d=out[-1]+NC+1
        out.append(-(-d//NC)*NC if k in (3,7) else d)
    return out


def ring_sizes(NC):
    F,U,D0,D1,D2,B2,B1,B0,V=range(9)
    life=[(F,V),(F,V),(U,B0),(D0,B1),(D1,B2),(U,B0),(D0,B1),(D1,B2),(U,B0),(D0,B1),(D1,B2),
          (D0,B0),(D1,B1),(D2,B2),(D0,B1),(D1,B2),(D2,B2),(B2,B1),(B1,B0),(B1,B0),(B2,B1),(D2,B2),(D2,V)]
    out=[]; lag=lags(NC)
    for w,r in life:
        need=lag[r]-lag[w]+NC+2
        out.append(max(8,1<<(need-1).bit_length()))
    return out


UN=2
VMEM=28


class Lay:
    def __init__(self, nd, nf):
        self.nd, self.nf, self.n = nd, nf, nd * nf
        self.wu, self.wd, self.wp, self.wr, self.wg = 128 // nf, 96 // nf, 32 // nf, 32 // nf, 64 // nf
        self.pu = 64 // nd // 8
        at = 0
        self.u = []
        for _ in range(self.pu):
            self.u.append(at)
            at += self.wu
        self.d = []
        for _ in range(3):
            self.d.append(at)
            at += self.wd
        self.p = []
        for _ in range(6):
            self.p.append(at)
            at += self.wp
        self.r = []
        for _ in range(3):
            self.r.append(at)
            at += self.wr
        self.g = at
        assert at + self.wg <= 128


def lane8(): return lax.broadcasted_iota(jnp.int32,(8,L),1)


def move(x, frm, to):
    k=(to-frm)%L
    return x if k==0 else pltpu.roll(x,k,1)


def put(acc, x, frm, to, w):
    lane=lane8()
    return jnp.where((lane>=to)&(lane<to+w),move(x,frm,to),acc)


def tap_perm():
    r=lax.broadcasted_iota(jnp.int32,(L,L),0); c=lax.broadcasted_iota(jnp.int32,(L,L),1)
    pos=((r&3)+3)&3
    return (c==pos*32+(r>>2)).astype(F32).astype(BF)


def square(x):
    return jnp.concatenate([x,jnp.zeros((L-x.shape[0],L),F32)],axis=0) if x.shape[0]<L else x


def prologue(lay, recv, wu, wv, wd, wdb, pa, bias, dirs, cols):
    nd,nf=lay.nd,lay.nf
    z=jnp.zeros((8,L),F32)
    lane=lane8()
    def pick(x, at, w, acc):
        at=at%L
        return jnp.where((lane>=at)&(lane<at+w),x,acc)
    def gather(i, o, w, count):
        acc=[z]*count
        for f in range(nf):
            x=move(recv[i*nf+f].astype(F32),o,f*w)
            acc=[pick(x,(f+q)*w,w,y) for q,y in enumerate(acc)]
        return acc
    ud=jnp.concatenate([move(x,p*lay.wu,0) for i in range(nd) for p,x in enumerate(gather(i,lay.u[0],lay.wu,lay.pu))],axis=0)
    dd=[[] for _ in range(3)]; pd=[[] for _ in range(3)]
    for i in range(nd):
        x=gather(i,lay.d[0],lay.wd,3); y=gather(i,lay.p[0],lay.wp,6)
        for b in range(3):
            dd[b].append(move(x[b],b*lay.wd,0))
            pd[b].append(move(y[2*b],2*b*lay.wp,0)+move(y[2*b+1],(2*b+1)*lay.wp,32))
    dd=[jnp.concatenate(x,axis=0) for x in dd]; pd=[jnp.concatenate(x,axis=0) for x in pd]
    sm=[move(x,b*lay.wr,0) for b,x in enumerate(gather(0,lay.r[0],lay.wr,3))]+gather(0,lay.g,lay.wg,1)+gather(0,lay.g,lay.wr,1)
    st=square(jnp.concatenate(sm,axis=0)).T
    def col(q,rows): return jnp.broadcast_to(st[:rows,q:q+1],(rows,L))
    def norm(x): return jnp.broadcast_to(jnp.sqrt(jnp.sum(x*x,axis=1,keepdims=True)),x.shape)
    n=norm(ud); g=col(24,64)
    dirs[0:64]=ud; cols[0,0:64]=g/n; cols[1,0:64]=1.0/n
    w=dot((g*ud/n).astype(BF),tap_perm())
    wv[...]=w.astype(BF)
    m=jnp.concatenate([w,pltpu.roll(w,64,1)],axis=0).T
    lane=lax.broadcasted_iota(jnp.int32,(32,L),1)
    z32=jnp.zeros((32,L),F32)
    def left(x): return jnp.where(lane<64,x,0.0)
    x=jnp.concatenate([jnp.concatenate([m[:32],z32],axis=1),
                       jnp.concatenate([left(m[32:64]),left(pltpu.roll(m[32:64],64,1))],axis=1)],axis=0)
    wu[...]=x[:,:192].astype(BF)
    bias[0]=col(33,32)
    for b in range(3):
        r=64+32*b
        x=dd[b]; n=norm(x); g=col(8*b,32)
        dirs[r:r+32]=x; cols[0,r:r+32]=g/n; cols[1,r:r+32]=1.0/n
        w=(g*x/n).astype(BF).astype(F32)
        wd[b]=w[:,:96].astype(BF)
        m=square(jnp.concatenate([pltpu.roll(w,64,1),pltpu.roll(w,96,1),w],axis=0)).T
        back=m[:32]
        r=160+32*b
        x=pd[b]
        n=jnp.where(lane<32,norm(jnp.where(lane<32,x,0.0)),norm(jnp.where(lane<32,0.0,x)))
        g=jnp.where(lane<32,col(8*b+1,32),col(8*b+2,32))
        dirs[r:r+32]=x; cols[0,r:r+32]=g/n; cols[1,r:r+32]=1.0/n
        w=(g*x/n).astype(BF)
        w=w.astype(F32)
        m=square(w).T
        wide=jnp.where(lane<32,m[:64][32:],0.0)
        wdb[b]=jnp.concatenate([back,pltpu.roll(wide,96,1)],axis=0).astype(BF)
        wide=jnp.where(lane<32,m[:32],0.0)
        pa[b]=jnp.concatenate([w,pltpu.roll(wide,64,1)],axis=0)[:,:96].astype(BF)
        bias[1+2*b]=col(8*b+3,32)
        bias[2+2*b]=col(8*b+4,32)+col(8*b+5,32)


def epilogue(lay, dU, dN, dB, dirs, cols, tmp, msgs):
    nd,nf=lay.nd,lay.nf
    def rs(x): return jnp.sum(x,axis=1,keepdims=True)
    lane=lax.broadcasted_iota(jnp.int32,(64,L),1); lane32=lane[:32]
    C=jnp.zeros((64,L),F32)
    def place(C,q,c):
        c=jnp.broadcast_to(c,(c.shape[0],L))
        if c.shape[0]==32: c=jnp.concatenate([c,jnp.zeros((32,L),F32)],axis=0)
        return jnp.where(lane==q,c,C)
    perm=tap_perm()
    v=dot(dirs[0:64].astype(BF),perm); w=dU[...].T[:64]; s=cols[0,0:64]; i=cols[1,0:64]
    inner=rs(w*v)
    C=place(C,24,inner*i)
    g=s*(w-(inner*i*i)*v)
    gu=dot_nt(g.astype(BF),perm)
    gd=[];gp=[]
    tmp[...]=jnp.zeros_like(tmp)
    for b in range(3):
        r=64+32*b
        for t in range(3): tmp[b,:,t*32:t*32+32]=dN[b,(2-t)*32:(3-t)*32,:32]
        v=dirs[r:r+32]; w=tmp[b]; s=cols[0,r:r+32]; i=cols[1,r:r+32]
        inner=rs(w*v)
        C=place(C,8*b,inner*i)
        gd.append(s*(w-(inner*i*i)*v))
        r=160+32*b
        tmp[3+b]=square(dN[b,96:160]).T[:32]
        v=dirs[r:r+32]; w=tmp[3+b]; s=cols[0,r:r+32]; i=cols[1,r:r+32]
        p=w*v
        inner=jnp.where(lane32<32,rs(jnp.where(lane32<32,p,0.0)),rs(jnp.where(lane32<32,0.0,p)))
        C=place(C,8*b+1,inner[:,:1]*i[:,:1])
        C=place(C,8*b+2,inner[:,32:33]*i[:,32:33])
        gp.append(s*(w-(inner*i*i)*v))
        C=place(C,8*b+3,rs(dB[b,0]))
        o=rs(dB[b,1])
        C=place(C,8*b+4,o); C=place(C,8*b+5,o)
    C=place(C,33,rs(dB[0,2]))
    S=square(C).T
    lane=lane8(); row=lax.broadcasted_iota(jnp.int32,(8,L),0)
    def join(xs, f, w, o):
        acc=xs[0]
        for q,x in enumerate(xs[1:],1):
            at=(f+q)*w%L
            acc=jnp.where((lane>=at)&(lane<at+w),x,acc)
        return move(acc,f*w,o)
    def upto(at, x, y): return jnp.where(lane<at,x,y)
    us=[[move(gu[(d*lay.pu+p)*8:(d*lay.pu+p)*8+8],0,p*lay.wu) for p in range(lay.pu)] for d in range(nd)]
    ds=[[move(gd[b][8*d:8*d+8],0,b*lay.wd) for b in range(3)] for d in range(nd)]
    ps=[[move(gp[q//2][8*d:8*d+8],32*(q%2),q*lay.wp) for q in range(6)] for d in range(nd)]
    rs_=[move(S[8*b:8*b+8],0,b*lay.wr) for b in range(3)]
    for f in range(nf):
        g=jnp.where(row==1,move(S[32:40],f*lay.wr,lay.g),move(S[24:32],f*lay.wg,lay.g))
        sm=upto(lay.g,join(rs_,f,lay.wr,lay.r[0]),jnp.where(lane<lay.g+lay.wg,g,0.0))
        for d in range(nd):
            x=upto(lay.d[0],join(us[d],f,lay.wu,lay.u[0]),
              upto(lay.p[0],join(ds[d],f,lay.wd,lay.d[0]),
              upto(lay.r[0],join(ps[d],f,lay.wp,lay.p[0]),sm)))
            msgs[d*nf+f]=x.astype(BF)


def make_masks(seg, masks, cpp):
    T=cpp*L
    s=seg[...]
    pos=lax.broadcasted_iota(jnp.int32,s.shape,1)
    for k,kind in KINDS.items():
        r=pltpu.roll(s,(-k)%T,1)
        m=((r==s)&(pos+k>=0)&(pos+k<T)).astype(F32)
        for p in range(s.shape[0]):
            mp=jnp.broadcast_to(m[p:p+1,:],(16,T)).astype(BF)
            for c in range(cpp): masks[p*cpp+c,kind]=mp[:,c*L:(c+1)*L]


def main_kernel(NC, packs, cpp, lay, sig, masks, cot, recv, out_h, sg_h, dU, dN, dB, dirs, cols,
                outb, sgb, bias, sem_out):
    def body(wu, wv, wd, wdb, pa, perm, *rings):
        make_perm(perm)
        main_body(NC,packs,cpp,lay,recv,wu,wv,wd,wdb,pa,bias,perm,out_h,sg_h,dU,dN,dB,
                  sig,cot,outb,sgb,dirs,cols,sem_out,masks,rings)
    pl.run_scoped(body,pltpu.VMEM((64,192),BF),pltpu.VMEM((64,L),BF),pltpu.VMEM((3,32,96),BF),pltpu.VMEM((3,64,L),BF),
                  pltpu.VMEM((3,64,96),BF),pltpu.VMEM((2*L,2*L),BF),
                  *[pltpu.VMEM((r,64,L),BF) for r in ring_sizes(NC)])


def main_body(NC, packs, cpp, lay, recv, wu, wv, wd, wdb, pa, bias, perm,
              out_h, sg_h, dU, dN, dB, sig, cot, outb, sgb, dirs, cols, sem_out, masks, rings):
    NCOL=packs*cpp
    (FIRST,DFIRST,PRE0,PRE1,PRE2,HID0,HID1,HID2,DH0,DH1,DH2,ACT0,ACT1,ACT2,DD0,DD1,G2,G1,G0,GD0,GD1,GD2,GU)=range(23)
    PRE=(PRE0,PRE1,PRE2);HID=(HID0,HID1,HID2);DH=(DH0,DH1,DH2);ACT=(ACT0,ACT1,ACT2);DD=(DD0,DD1);GD=(GD0,GD1,GD2);G=(G0,G1,G2)
    dl=lags(NC)
    sizes=ring_sizes(NC)
    assert cpp%NC==0 and dl[4]%NC==0 and dl[8]%NC==0
    def copy_out_y(p): return pltpu.make_async_copy(outb.at[p],out_h.at[p],sem_out.at[0,p])
    def copy_out_x(p): return pltpu.make_async_copy(sgb.at[p],sg_h.at[p],sem_out.at[1,p])
    def copies_out(p): return copy_out_y(p),copy_out_x(p)
    dU[...]=jnp.zeros_like(dU); dN[...]=jnp.zeros_like(dN); dB[...]=jnp.zeros_like(dB)
    for r,q in zip(sizes,rings):
        n=min(r,dl[8]-dl[4]+4)
        q[pl.ds(r-n,n)]=jnp.zeros((n,64,L),BF)
    prologue(lay,recv,wu,wv,wd,wdb,pa,bias,dirs,cols)
    def slot(r,j): return j & (sizes[r]-1)
    def ld(r,j0,n):
        return jnp.concatenate([rings[r][slot(r,j0+k)] for k in range(n)],axis=1) if n>1 else rings[r][slot(r,j0)]
    def st(r,j0,v):
        v=v.astype(BF)
        for k in range(v.shape[1]//L): rings[r][slot(r,j0+k)]=v[:,k*L:(k+1)*L]
    def clampj(j): return min(max(j,0),NCOL-1) if isinstance(j,int) else jnp.clip(j,0,NCOL-1)
    def mult(x): return x if isinstance(x,int) else pl.multiple_of(x,NC*L)
    def cat0(*v): return jnp.concatenate(v,axis=0)
    def mask(kind,j0,rows,n):
        cols=[]
        for k in range(n):
            m=masks[clampj(j0+k),KINDS[kind]]
            cols.append(jnp.concatenate([m]*(rows//16),axis=0))
        return jnp.concatenate(cols,axis=1)
    def shf(x,k):
        W=x.shape[1]-2*L
        if k>0: return pltpu.roll(x[:,L:],W+L-k,1)[:,:W]
        return pltpu.roll(x[:,:W+L],-k,1)[:,L:]
    def stack(r,j0,n,b):
        x=ld(r,j0-1,n+2)
        E=x[:32]; O=x[32:]
        a_=(3**b-1)//2; b_=(3**b+1)//2
        Em=E[:,L:L+n*L]; Om=O[:,L:L+n*L]
        Omin=shf(O,-b_)*mask(-b_,j0,32,n)
        Opl=shf(O,a_)*mask(a_,j0,32,n) if a_ else Om
        Emin=shf(E,-a_)*mask(-a_,j0,32,n) if a_ else Em
        Epl=shf(E,b_)*mask(b_,j0,32,n)
        return jnp.concatenate([Omin,Em,Opl],axis=0),jnp.concatenate([Emin,Om,Epl],axis=0)
    def per_phase(w,xE,xO): return jnp.concatenate([dot(w,xE),dot(w,xO)],axis=0)
    def rowsum(v):
        s=v[:32]+v[32:]
        r=s[:,:L]
        for k in range(1,v.shape[1]//L): r=r+s[:,k*L:(k+1)*L]
        return r
    def biased(x,i):
        y=jnp.concatenate([bias[i]]*(x.shape[1]//L),axis=1)
        return x+jnp.concatenate([y,y],axis=0)
    def pc(j):
        jc=clampj(j)
        return (jc//cpp,jc%cpp) if isinstance(j,int) else (lax.div(jc,cpp),lax.rem(jc,cpp))
    def po(j):
        if isinstance(j,int): return pc(j)
        return jnp.where(j>=0,lax.div(clampj(j),cpp),packs), lax.rem(clampj(j),cpp)
    def stages(at, n):
        X={}
        jv=at[8]; jb=[at[7],at[6],at[5]]; jd=[at[2],at[3],at[4]]; ju=at[1]; jf=at[0]
        W=n*L
        def V1():
            x=ld(GU,jv-1,n+2)
            gt=cat0(x[:,L:L+W], shf(x[:32],1)*mask(1,jv,32,n), shf(x[32:],-1)*mask(-1,jv,32,n))
            y=dot(wv[...],gt)
            dU[:,:64]+=dot_nt(gt,ld(FIRST,jv,n))
            p,c=po(jv)
            sgb[p,:,pl.ds(mult(c*L),W)]=((0.2*y)*ld(DFIRST,jv,n).astype(F32)).astype(BF)
        def NT(b):
            g=ld(G[b],jb[b],n); act=ld(ACT[b],jb[b],n); hid=ld(HID[b],jb[b],n)
            dN[b,96:,:32]+=dot_nt(cat0(act[:32],hid[:32]),g[:32])+dot_nt(cat0(act[32:],hid[32:]),g[32:])
        def A(b):
            e,o=stack(GD[b],jb[b],n,b)
            g=ld(G[b],jb[b],n)
            X['A',b]=dot(wdb[b],cat0(e,g[:32])),dot(wdb[b],cat0(o,g[32:]))
            pre=ld(PRE[b],jb[b],n)
            dN[b,:96,:32]+=dot_nt(e,pre[:32])+dot_nt(o,pre[32:])
        def B2(b):
            x,y=X['A',b]
            gf=ld(DH[b],jb[b],n).astype(F32)*(0.2*cat0(x[:32],y[:32]))+cat0(x[32:],y[32:])
            gl=gf.astype(BF)
            if b==0:
                st(GU,jb[b],gl); dB[0,2]+=rowsum(gf)
            else:
                st(G[b-1],jb[b],gl); dB[b-1,1]+=rowsum(gf)
                X['g',b-1]=gl
        def AG(b):
            g=X['g',b]
            X['ag',b]=per_phase(pa[b,32:,64:],g[:32],g[32:])
        def PW(b):
            a=X['act',b]; h=ld(HID[b],jd[b],n)
            X['h',b]=per_phase(pa[b,:32,:64],cat0(a[:32],h[:32]),cat0(a[32:],h[32:]))
        def PA(b):
            a=X['act',b]; h=ld(HID[b],jd[b],n); g=X['g',b]
            x=dot(pa[b],cat0(a[:32],h[:32],g[:32])); y=dot(pa[b],cat0(a[32:],h[32:],g[32:]))
            X['h',b]=cat0(x[:32],y[:32]); X['ag',b]=cat0(x[32:],y[32:])
        def B3(b):
            gd=ld(DD[b-1],jb[b],n).astype(F32)*(0.2*X['ag',b-1])
            dB[b-1,0]+=rowsum(gd)
            st(GD[b-1],jb[b],gd)
        def D1(b):
            X['dil',b]=per_phase(wd[b],*stack(PRE[b],jd[b],n,b))
        def D2(b):
            act,dd=act_pair(biased(X['dil',b],1+2*b))
            act=act.astype(BF)
            st(ACT[b],jd[b],act)
            if b<2: st(DD[b],jd[b],dd)
            else: X['dd']=dd
            X['act',b]=act
        def G2f():
            p,c=pc(jd[2])
            gl=cot[p,:,pl.ds(mult(c*L),W)]
            st(G2,jd[2],gl)
            dB[2,1]+=rowsum(gl.astype(F32))
            X['g',2]=gl
        def D3(b):
            h=biased(X['h',b],2+2*b)
            if b<2:
                pre,dh=act_pair(h)
                st(PRE[b+1],jd[b],pre); st(HID[b+1],jd[b],h); st(DH[b+1],jd[b],dh)
            else:
                ho=h.astype(BF)
                z=cat0(*[jnp.concatenate([ho[:32,k*L:(k+1)*L],ho[32:,k*L:(k+1)*L]],axis=1) for k in range(n)])
                X['z']=dot(z,perm[...])
        def GD2f():
            gd=X['dd'].astype(F32)*(0.2*X['ag',2])
            dB[2,0]+=rowsum(gd)
            st(GD2,jd[2],gd)
        def O():
            z=X['z'].astype(BF)
            p,c=pc(jd[2])
            outb[p,:,pl.ds(mult(c*2*L),2*W)]=jnp.concatenate([z[k*32:(k+1)*32] for k in range(n)],axis=1)
        def U1():
            x=ld(FIRST,ju-1,n+2)
            fm=shf(x,-1)*mask(-1,ju,64,n); fp=shf(x,1)*mask(1,ju,64,n)
            X['u']=dot(wu[...],cat0(x[:,L:L+W],fm,fp))
        def U2():
            h=biased(X['u'],0)
            pre,dh=act_pair(h)
            st(PRE0,ju,pre); st(HID0,ju,h); st(DH0,ju,dh)
        def F():
            p,c=pc(jf if isinstance(jf,int) else jnp.minimum(jf,NCOL-n))
            fv,dv=act_pair(sig[p,:,pl.ds(mult(c*L),W)])
            st(FIRST,jf,fv); st(DFIRST,jf,dv)
        return {k: v for k,v in locals().items() if k in NAMES}
    def step(i):
        FULL(stages([i*NC-d for d in dl],NC))
    def chunks(first,end):
        return [(j,min(NC,end-j)) for j in range(first,end,NC)]
    def sweep(k,first,end,*calls):
        parts=[stages([j]*9,n) for j,n in chunks(first,end)]
        for call in calls:
            for e in parts: call(e)
    first=dl[4]//NC; last=first+NCOL//NC
    ipp=cpp//NC
    sweep(0,0,first*NC,lambda e: e["F"]())
    sweep(1,0,first*NC-dl[1],lambda e: e["U1"](),lambda e: e["U2"]())
    for b in range(2):
        sweep(2+b,0,first*NC-dl[2+b],lambda e: e["D1"](b),lambda e: e["D2"](b),lambda e: e["PW"](b),lambda e: e["D3"](b))
    done=-(-dl[8]//NC)+ipp
    assert (last-first)%UN==0
    def full(g,c):
        i=first+g*UN
        for k in range(UN):
            @pl.when((lax.rem(i-k,ipp)==done%ipp)&(i-k>=done))
            def _():
                for q in copies_out(lax.div(i-k-done,ipp)): q.start()
        for k in range(UN): step(i+k)
        return c
    lax.fori_loop(0,(last-first)//UN,full,0)
    begun=[first+g*UN-k for g in range((last-first)//UN) for k in range(UN)]
    started=[p for p in range(packs) if p*ipp+done in begun]
    out_left=range(len(started),packs)
    for p in out_left: copy_out_y(p).start()
    for b in (2,1):
        sweep(7-b,last*NC-dl[7-b],NCOL,lambda e: e["A"](b),lambda e: e["NT"](b),lambda e: e["B2"](b),lambda e: e["AG"](b-1),lambda e: e["B3"](b))
    sweep(7,last*NC-dl[7],NCOL,lambda e: e["A"](0),lambda e: e["NT"](0),lambda e: e["B2"](0))
    sweep(8,last*NC-dl[8],NCOL,lambda e: e["V1"]())
    for p in out_left: copy_out_x(p).start()
    for p in range(packs):
        for c in copies_out(p): c.wait()


def make_perm(perm, back=False):
    r=lax.broadcasted_iota(jnp.int32,(2*L,2*L),0); c=lax.broadcasted_iota(jnp.int32,(2*L,2*L),1)
    to=lambda x: jnp.where(x<L,2*x,2*(x-L)+1)
    perm[...]=((to(c)==r) if back else (to(r)==c)).astype(F32).astype(BF)


def main_call(NC, lay, signal, masks, cot, recv):
    packs,cin,T=signal.shape
    cpp=T//L
    V=pl.BlockSpec(memory_space=pltpu.VMEM); A=pl.BlockSpec(memory_space=pl.ANY)
    return pl.pallas_call(
        functools.partial(main_kernel,NC,packs,cpp,lay),
        name="section",
        out_shape=(jax.ShapeDtypeStruct((packs,32,2*T),BF),jax.ShapeDtypeStruct(signal.shape,BF),
            *[jax.ShapeDtypeStruct(x,F32) for x in ((L,L),(3,160,L),(3,3,32,L),(256,L),(2,256,L))]),
        in_specs=[V]*4, out_specs=(A,A,V,V,V,V,V),
        scratch_shapes=[pltpu.VMEM((packs,32,2*T),BF),pltpu.VMEM((packs+1,64,T),BF),
            pltpu.VMEM((7,32,L),F32),
            pltpu.SemaphoreType.DMA((2,packs))],
        compiler_params=pltpu.CompilerParams(vmem_limit_bytes=VMEM<<20),
    )(signal,masks,cot,recv)

from jax.sharding import PartitionSpec as P

MESH = pl.DeviceIdType.MESH


def peer(lay, k):
    me = lax.axis_index("dp") * lay.nf + lax.axis_index("fsdp")
    t = lax.rem(me + k, lay.n)
    return me, t, {"dp": t // lay.nf, "fsdp": lax.rem(t, lay.nf)}


def greet(lay):
    barrier = pltpu.get_barrier_semaphore()

    def hello(k, c):
        _, _, dev = peer(lay, k)
        pl.semaphore_signal(barrier, inc=1, device_id=dev, device_id_type=MESH)
        return c

    lax.fori_loop(1, lay.n, hello, 0)
    return barrier


def copy_out(lay, source, recv, send_sem, recv_sem, k):
    me, t, dev = peer(lay, k)
    return pltpu.make_async_remote_copy(
        src_ref=source(t), dst_ref=recv.at[me], send_sem=send_sem.at[k], recv_sem=recv_sem.at[k],
        device_id=dev, device_id_type=MESH)


def send(lay, *args):
    def start(k, c):
        copy_out(lay, *args, k).start()
        return c

    lax.fori_loop(1, lay.n, start, 0)


def receive(lay, *args):
    def finish(k, c):
        copy_out(lay, *args, k).wait()
        return c

    lax.fori_loop(1, lay.n, finish, 0)


def gather_kernel(lay, cot_h, *refs):
    shards_h, seg_h, (out, split, masks), shards = refs[:7], refs[7], refs[8:11], refs[11:18]
    acc, sq, msg, recv, perm, cot, seg, send_sem, recv_sem, in_sem, seg_sem, shard_sem = refs[18:]
    packs, _, width = cot_h.shape
    load = [pltpu.make_async_copy(h, v, shard_sem.at[k]) for k, (h, v) in enumerate(zip(shards_h, shards)) if v.size > 1]
    shards = [h if h.size == 1 else v for h, v in zip(shards_h, shards)]
    fetch = [pltpu.make_async_copy(cot_h.at[p], cot.at[p], in_sem.at[p]) for p in range(packs)]
    barrier = greet(lay)
    count = pltpu.make_async_copy(seg_h, seg, seg_sem)
    for c in load + [count] + fetch:
        c.start()
    acc[...] = jnp.zeros_like(acc)
    sq[...] = jnp.zeros_like(sq)
    for c in load:
        c.wait()
    ud, dd, pd, ug, ub, rg, rb = shards
    for p, o in enumerate(lay.u):
        acc[:, o:o + lay.wu] = ud[8 * p:8 * p + 8].astype(F32)
    for b in range(3):
        acc[:, lay.d[b]:lay.d[b] + lay.wd] = dd[b].astype(F32)
        for j in range(2):
            o = (2 * b + j) * lay.wp
            sq[o:o + lay.wp, 0:8] = pd[b, j].astype(F32)
        o = lay.r[b]
        acc[0:3, o:o + lay.wr] = rg[b].astype(F32)
        acc[3:6, o:o + lay.wr] = rb[b].astype(F32)
    acc[0:1, lay.g:lay.g + lay.wg] = ug[...].astype(F32)
    acc[1:2, lay.g:lay.g + lay.wr] = ub[...].astype(F32)
    full = put(acc[...], sq[...].T[:8], 0, lay.p[0], 6 * lay.wp).astype(BF)
    msg[...] = full
    me = peer(lay, 0)[0]
    recv[me] = full
    step = 8

    def part(p):
        fetch[p].wait()
        for k in range(0, width // (2 * L), step):
            x = jnp.concatenate([cot[p, :, (k + q) * 2 * L:(k + q + 1) * 2 * L] for q in range(step)], axis=0)
            z = dot(x, perm[...]).astype(BF)
            for e in range(2):
                y = jnp.concatenate([z[q * 32:(q + 1) * 32, e * L:(e + 1) * L] for q in range(step)], axis=1)
                split[p, e * 32:(e + 1) * 32, k * L:(k + step) * L] = y

    pl.semaphore_wait(barrier, lay.n - 1)
    args = (lambda t: msg, recv, send_sem, recv_sem)
    send(lay, *args)
    count.wait()
    make_masks(seg, masks, width // (2 * L))
    make_perm(perm, True)
    for p in range(packs):
        part(p)
    receive(lay, *args)
    out[...] = recv[...]


def scatter_kernel(lay, dU, dN, dB, dirs, cols, out, tmp, msgs, recv, send_sem, recv_sem):
    barrier = greet(lay)
    epilogue(lay, dU, dN, dB, dirs, cols, tmp, msgs)
    me = peer(lay, 0)[0]
    recv[me] = msgs[me]
    pl.semaphore_wait(barrier, lay.n - 1)
    args = (lambda t: msgs.at[t], recv, send_sem, recv_sem)
    send(lay, *args)
    receive(lay, *args)
    out[...] = recv[...]


def sum_kernel(lay, recv, gud, gug, gub, gdd, gpd, grg, grb):
    t = recv[0].astype(F32)
    for s in range(1, lay.n):
        t = t + recv[s].astype(F32)
    m = jnp.concatenate([move(t, lay.p[0], 0), jnp.zeros((L - 8, L), F32)], axis=0).T
    for p, o in enumerate(lay.u):
        gud[8 * p:8 * p + 8] = t[:, o:o + lay.wu]
    for b in range(3):
        gdd[b] = t[:, lay.d[b]:lay.d[b] + lay.wd]
        for j in range(2):
            o = (2 * b + j) * lay.wp
            gpd[b, j] = m[o:o + lay.wp, 0:8]
        o = lay.r[b]
        grg[b] = t[0:3, o:o + lay.wr]
        grb[b] = t[3:6, o:o + lay.wr]
    gug[...] = t[0:1, lay.g:lay.g + lay.wg]
    gub[...] = t[1:2, lay.g:lay.g + lay.wr]


def per_device(lay, signal, segments, cotangent, ud, ug, ub, dd, pd, rg, rb):
    V = pl.BlockSpec(memory_space=pltpu.VMEM)
    tiles = jax.ShapeDtypeStruct((lay.n, 8, L), BF)
    sems = [pltpu.SemaphoreType.DMA((lay.n,)), pltpu.SemaphoreType.DMA((lay.n,))]
    packs, _, width = cotangent.shape
    parted = (packs, 64, width // 2)
    H = pl.BlockSpec(memory_space=pltpu.HBM)
    shards = (ud, dd, pd.transpose(0, 1, 3, 2), ug.reshape(1, -1), ub.reshape(1, -1), rg, rb)
    table, split, masks = pl.pallas_call(
        functools.partial(gather_kernel, lay), name="gather_params", out_shape=(tiles, jax.ShapeDtypeStruct(parted, BF), jax.ShapeDtypeStruct((packs * width // (2 * L), 8, 16, L), BF)),
        in_specs=[H] + [H if v.size > 1 else V for v in shards] + [H], out_specs=(V, V, V),
        scratch_shapes=[pltpu.VMEM(v.shape, v.dtype) for v in shards] + [pltpu.VMEM((8, L), F32), pltpu.VMEM((L, L), F32), pltpu.VMEM((8, L), BF), pltpu.VMEM((lay.n, 8, L), BF),
                        pltpu.VMEM((2 * L, 2 * L), BF), pltpu.VMEM(cotangent.shape, BF), pltpu.VMEM(segments.shape, jnp.int32)] + sems
        + [pltpu.SemaphoreType.DMA((packs,)), pltpu.SemaphoreType.DMA, pltpu.SemaphoreType.DMA((7,))],
        compiler_params=pltpu.CompilerParams(collective_id=0, has_side_effects=True, vmem_limit_bytes=20 << 20),
    )(*(pltpu.with_memory_space_constraint(v, pltpu.HBM) if v.size > 1 else v for v in (cotangent, *shards, segments)))
    out, sg, *sums = main_call(NC, lay, signal, masks, split, table)
    got = pl.pallas_call(
        functools.partial(scatter_kernel, lay), name="scatter_grads", out_shape=tiles,
        in_specs=[V] * 5, out_specs=V,
        scratch_shapes=[pltpu.VMEM((6, 32, L), F32), pltpu.VMEM((lay.n, 8, L), BF), pltpu.VMEM((lay.n, 8, L), BF)] + sems,
        compiler_params=pltpu.CompilerParams(collective_id=1, has_side_effects=True, vmem_limit_bytes=4 << 20),
    )(*sums)
    f = lambda *s: jax.ShapeDtypeStruct(s, F32)
    gud, gug, gub, gdd, gpd, grg, grb = pl.pallas_call(
        functools.partial(sum_kernel, lay), name="sum_grads",
        out_shape=(f(*ud.shape), f(1, ug.shape[0]), f(1, ub.shape[0]), f(*dd.shape), f(3, 2, pd.shape[3], pd.shape[2]), f(*rg.shape), f(*rb.shape)),
        in_specs=[V], out_specs=(V,) * 7,
        compiler_params=pltpu.CompilerParams(vmem_limit_bytes=2 << 20),
    )(got)
    return out, sg, gud, gug.reshape(-1), gub.reshape(-1), gdd, gpd.transpose(0, 1, 3, 2), grg, grb


NC = 4


def solution(mesh):
    lay = Lay(mesh.shape["dp"], mesh.shape["fsdp"])
    return jax.shard_map(
        functools.partial(per_device, lay),
        mesh=mesh,
        in_specs=(
            P(("dp", "fsdp"), None, None),
            P(("dp", "fsdp"), None),
            P(("dp", "fsdp"), None, None),
            P("dp", "fsdp"),
            P("fsdp"),
            P("fsdp"),
            P(None, "dp", "fsdp"),
            P(None, None, "dp", "fsdp"),
            P(None, None, "fsdp"),
            P(None, None, "fsdp"),
        ),
        out_specs=(
            P(("dp", "fsdp"), None, None),
            P(("dp", "fsdp"), None, None),
            P("dp", "fsdp"),
            P("fsdp"),
            P("fsdp"),
            P(None, "dp", "fsdp"),
            P(None, None, "dp", "fsdp"),
            P(None, None, "fsdp"),
            P(None, None, "fsdp"),
        ),
        check_vma=False,
    )
```

```python
import functools
import jax, jax.numpy as jnp
from jax import lax
from jax.experimental import pallas as pl
from jax.experimental.pallas import tpu as pltpu

BF=jnp.bfloat16; F32=jnp.float32
L=128

def dot(a,b):
    return jnp.dot(a,b,preferred_element_type=F32)
def dot_nt(a,b):
    return lax.dot_general(a,b,(((1,),(1,)),((),())),preferred_element_type=F32)

def act_pair(h):
    h=h.astype(F32)
    v=h.astype(BF); w=(0.2*h).astype(BF)
    c=lambda x: jnp.asarray(x,BF)
    th=jnp.tanh(c(0.5)*v); t=c(3.0)+c(2.0)*th; q=c(1.0)-th*th
    return w*t, t+v*q

KINDS={-1:0,1:1,-2:2,2:3,-4:4,4:5,-5:6,5:7}

NAMES=("V1","NT","A","B2","AG","PW","PA","B3","D1","D2","G2f","D3","GD2f","O","U1","U2","F")


def FULL(e):
    V1,NT,A,B2,AG,PW,PA,B3,D1,D2,G2f,D3,GD2f,O,U1,U2,F=[e[k] for k in NAMES]
    G2f(); D1(2); NT(2); D2(2); A(2); D1(1); NT(1); PA(2)
    A(1); V1(); D1(0); D2(1); B2(2); PA(1); B3(2); GD2f()
    D3(2); B2(1); D2(0); F(); A(0); PA(0); U1(); O()
    NT(0); B3(1); D3(1); D3(0); B2(0); U2()


def lags(NC):
    out=[0]
    for k in range(8):
        d=out[-1]+NC+1
        out.append(-(-d//NC)*NC if k in (3,7) else d)
    return out


def ring_sizes(NC):
    F,U,D0,D1,D2,B2,B1,B0,V=range(9)
    life=[(F,V),(F,V),(U,B0),(D0,B1),(D1,B2),(U,B0),(D0,B1),(D1,B2),(U,B0),(D0,B1),(D1,B2),
          (D0,B0),(D1,B1),(D2,B2),(D0,B1),(D1,B2),(D2,B2),(B2,B1),(B1,B0),(B1,B0),(B2,B1),(D2,B2),(D2,V)]
    out=[]; lag=lags(NC)
    for w,r in life:
        need=lag[r]-lag[w]+NC+2
        out.append(max(8,1<<(need-1).bit_length()))
    return out


UN=8
VMEM=28


class Lay:
    def __init__(self, nd, nf):
        self.nd, self.nf, self.n = nd, nf, nd * nf
        self.wu, self.wd, self.wp, self.wr, self.wg = 128 // nf, 96 // nf, 32 // nf, 32 // nf, 64 // nf
        self.pu = 64 // nd // 8
        at = 0
        self.u = []
        for _ in range(self.pu):
            self.u.append(at)
            at += self.wu
        self.d = []
        for _ in range(3):
            self.d.append(at)
            at += self.wd
        self.p = []
        for _ in range(6):
            self.p.append(at)
            at += self.wp
        self.r = []
        for _ in range(3):
            self.r.append(at)
            at += self.wr
        self.g = at
        assert at + self.wg <= 128


def lane8(): return lax.broadcasted_iota(jnp.int32,(8,L),1)


def move(x, frm, to):
    k=(to-frm)%L
    return x if k==0 else pltpu.roll(x,k,1)


def put(acc, x, frm, to, w):
    lane=lane8()
    return jnp.where((lane>=to)&(lane<to+w),move(x,frm,to),acc)


def tap_perm():
    r=lax.broadcasted_iota(jnp.int32,(L,L),0); c=lax.broadcasted_iota(jnp.int32,(L,L),1)
    pos=((r&3)+3)&3
    return (c==pos*32+(r>>2)).astype(F32).astype(BF)


def square(x):
    return jnp.concatenate([x,jnp.zeros((L-x.shape[0],L),F32)],axis=0) if x.shape[0]<L else x


def prologue(lay, recv, wu, wv, wd, wdb, pa, bias, dirs, cols):
    nd,nf=lay.nd,lay.nf
    z=jnp.zeros((8,L),F32)
    lane=lane8()
    def pick(x, at, w, acc):
        at=at%L
        return jnp.where((lane>=at)&(lane<at+w),x,acc)
    def gather(i, o, w, count):
        acc=[z]*count
        for f in range(nf):
            x=move(recv[i*nf+f].astype(F32),o,f*w)
            acc=[pick(x,(f+q)*w,w,y) for q,y in enumerate(acc)]
        return acc
    ud=jnp.concatenate([move(x,p*lay.wu,0) for i in range(nd) for p,x in enumerate(gather(i,lay.u[0],lay.wu,lay.pu))],axis=0)
    dd=[[] for _ in range(3)]; pd=[[] for _ in range(3)]
    for i in range(nd):
        x=gather(i,lay.d[0],lay.wd,3); y=gather(i,lay.p[0],lay.wp,6)
        for b in range(3):
            dd[b].append(move(x[b],b*lay.wd,0))
            pd[b].append(move(y[2*b],2*b*lay.wp,0)+move(y[2*b+1],(2*b+1)*lay.wp,32))
    dd=[jnp.concatenate(x,axis=0) for x in dd]; pd=[jnp.concatenate(x,axis=0) for x in pd]
    sm=[move(x,b*lay.wr,0) for b,x in enumerate(gather(0,lay.r[0],lay.wr,3))]+gather(0,lay.g,lay.wg,1)+gather(0,lay.g,lay.wr,1)
    st=square(jnp.concatenate(sm,axis=0)).T
    def col(q,rows): return jnp.broadcast_to(st[:rows,q:q+1],(rows,L))
    def norm(x): return jnp.broadcast_to(jnp.sqrt(jnp.sum(x*x,axis=1,keepdims=True)),x.shape)
    n=norm(ud); g=col(24,64)
    dirs[0:64]=ud; cols[0,0:64]=g/n; cols[1,0:64]=1.0/n
    w=dot((g*ud/n).astype(BF),tap_perm())
    wv[...]=w.astype(BF)
    m=jnp.concatenate([w,pltpu.roll(w,64,1)],axis=0).T
    lane=lax.broadcasted_iota(jnp.int32,(32,L),1)
    z32=jnp.zeros((32,L),F32)
    def left(x): return jnp.where(lane<64,x,0.0)
    x=jnp.concatenate([jnp.concatenate([m[:32],z32],axis=1),
                       jnp.concatenate([left(m[32:64]),left(pltpu.roll(m[32:64],64,1))],axis=1)],axis=0)
    wu[...]=x[:,:192].astype(BF)
    bias[0]=col(33,32)
    for b in range(3):
        r=64+32*b
        x=dd[b]; n=norm(x); g=col(8*b,32)
        dirs[r:r+32]=x; cols[0,r:r+32]=g/n; cols[1,r:r+32]=1.0/n
        w=(g*x/n).astype(BF).astype(F32)
        wd[b]=w[:,:96].astype(BF)
        m=square(jnp.concatenate([pltpu.roll(w,64,1),pltpu.roll(w,96,1),w],axis=0)).T
        back=m[:32]
        r=160+32*b
        x=pd[b]
        n=jnp.where(lane<32,norm(jnp.where(lane<32,x,0.0)),norm(jnp.where(lane<32,0.0,x)))
        g=jnp.where(lane<32,col(8*b+1,32),col(8*b+2,32))
        dirs[r:r+32]=x; cols[0,r:r+32]=g/n; cols[1,r:r+32]=1.0/n
        w=(g*x/n).astype(BF)
        w=w.astype(F32)
        m=square(w).T
        wide=jnp.where(lane<32,m[:64][32:],0.0)
        wdb[b]=jnp.concatenate([back,pltpu.roll(wide,96,1)],axis=0).astype(BF)
        wide=jnp.where(lane<32,m[:32],0.0)
        pa[b]=jnp.concatenate([w,pltpu.roll(wide,64,1)],axis=0)[:,:96].astype(BF)
        bias[1+2*b]=col(8*b+3,32)
        bias[2+2*b]=col(8*b+4,32)+col(8*b+5,32)


def epilogue(lay, dU, dN, dB, dirs, cols, tmp, msgs):
    nd,nf=lay.nd,lay.nf
    def rs(x): return jnp.sum(x,axis=1,keepdims=True)
    lane=lax.broadcasted_iota(jnp.int32,(64,L),1); lane32=lane[:32]
    C=jnp.zeros((64,L),F32)
    def place(C,q,c):
        c=jnp.broadcast_to(c,(c.shape[0],L))
        if c.shape[0]==32: c=jnp.concatenate([c,jnp.zeros((32,L),F32)],axis=0)
        return jnp.where(lane==q,c,C)
    perm=tap_perm()
    v=dot(dirs[0:64].astype(BF),perm); w=dU[...].T[:64]; s=cols[0,0:64]; i=cols[1,0:64]
    inner=rs(w*v)
    C=place(C,24,inner*i)
    g=s*(w-(inner*i*i)*v)
    gu=dot_nt(g.astype(BF),perm)
    gd=[];gp=[]
    tmp[...]=jnp.zeros_like(tmp)
    for b in range(3):
        r=64+32*b
        for t in range(3): tmp[b,:,t*32:t*32+32]=dN[b,(2-t)*32:(3-t)*32,:32]
        v=dirs[r:r+32]; w=tmp[b]; s=cols[0,r:r+32]; i=cols[1,r:r+32]
        inner=rs(w*v)
        C=place(C,8*b,inner*i)
        gd.append(s*(w-(inner*i*i)*v))
        r=160+32*b
        tmp[3+b]=square(dN[b,96:160]).T[:32]
        v=dirs[r:r+32]; w=tmp[3+b]; s=cols[0,r:r+32]; i=cols[1,r:r+32]
        p=w*v
        inner=jnp.where(lane32<32,rs(jnp.where(lane32<32,p,0.0)),rs(jnp.where(lane32<32,0.0,p)))
        C=place(C,8*b+1,inner[:,:1]*i[:,:1])
        C=place(C,8*b+2,inner[:,32:33]*i[:,32:33])
        gp.append(s*(w-(inner*i*i)*v))
        C=place(C,8*b+3,rs(dB[b,0]))
        o=rs(dB[b,1])
        C=place(C,8*b+4,o); C=place(C,8*b+5,o)
    C=place(C,33,rs(dB[0,2]))
    S=square(C).T
    lane=lane8(); row=lax.broadcasted_iota(jnp.int32,(8,L),0)
    def join(xs, f, w, o):
        acc=xs[0]
        for q,x in enumerate(xs[1:],1):
            at=(f+q)*w%L
            acc=jnp.where((lane>=at)&(lane<at+w),x,acc)
        return move(acc,f*w,o)
    def upto(at, x, y): return jnp.where(lane<at,x,y)
    us=[[move(gu[(d*lay.pu+p)*8:(d*lay.pu+p)*8+8],0,p*lay.wu) for p in range(lay.pu)] for d in range(nd)]
    ds=[[move(gd[b][8*d:8*d+8],0,b*lay.wd) for b in range(3)] for d in range(nd)]
    ps=[[move(gp[q//2][8*d:8*d+8],32*(q%2),q*lay.wp) for q in range(6)] for d in range(nd)]
    rs_=[move(S[8*b:8*b+8],0,b*lay.wr) for b in range(3)]
    for f in range(nf):
        g=jnp.where(row==1,move(S[32:40],f*lay.wr,lay.g),move(S[24:32],f*lay.wg,lay.g))
        sm=upto(lay.g,join(rs_,f,lay.wr,lay.r[0]),jnp.where(lane<lay.g+lay.wg,g,0.0))
        for d in range(nd):
            x=upto(lay.d[0],join(us[d],f,lay.wu,lay.u[0]),
              upto(lay.p[0],join(ds[d],f,lay.wd,lay.d[0]),
              upto(lay.r[0],join(ps[d],f,lay.wp,lay.p[0]),sm)))
            msgs[d*nf+f]=x.astype(BF)


def make_masks(seg, masks, cpp):
    T=cpp*L
    s=seg[...]
    pos=lax.broadcasted_iota(jnp.int32,s.shape,1)
    for k,kind in KINDS.items():
        r=pltpu.roll(s,(-k)%T,1)
        m=((r==s)&(pos+k>=0)&(pos+k<T)).astype(F32)
        for p in range(s.shape[0]):
            mp=jnp.broadcast_to(m[p:p+1,:],(16,T)).astype(BF)
            for c in range(cpp): masks[p*cpp+c,kind]=mp[:,c*L:(c+1)*L]


def main_kernel(NC, packs, cpp, lay, sig, masks, cot, recv, out_h, sg_h, dU, dN, dB, dirs, cols,
                outb, sgb, bias, sem_out):
    def body(wu, wv, wd, wdb, pa, perm, *rings):
        make_perm(perm)
        main_body(NC,packs,cpp,lay,recv,wu,wv,wd,wdb,pa,bias,perm,out_h,sg_h,dU,dN,dB,
                  sig,cot,outb,sgb,dirs,cols,sem_out,masks,rings)
    pl.run_scoped(body,pltpu.VMEM((64,192),BF),pltpu.VMEM((64,L),BF),pltpu.VMEM((3,32,96),BF),pltpu.VMEM((3,64,L),BF),
                  pltpu.VMEM((3,64,96),BF),pltpu.VMEM((2*L,2*L),BF),
                  *[pltpu.VMEM((r,64,L),BF) for r in ring_sizes(NC)])


def main_body(NC, packs, cpp, lay, recv, wu, wv, wd, wdb, pa, bias, perm,
              out_h, sg_h, dU, dN, dB, sig, cot, outb, sgb, dirs, cols, sem_out, masks, rings):
    NCOL=packs*cpp
    (FIRST,DFIRST,PRE0,PRE1,PRE2,HID0,HID1,HID2,DH0,DH1,DH2,ACT0,ACT1,ACT2,DD0,DD1,G2,G1,G0,GD0,GD1,GD2,GU)=range(23)
    PRE=(PRE0,PRE1,PRE2);HID=(HID0,HID1,HID2);DH=(DH0,DH1,DH2);ACT=(ACT0,ACT1,ACT2);DD=(DD0,DD1);GD=(GD0,GD1,GD2);G=(G0,G1,G2)
    dl=lags(NC)
    sizes=ring_sizes(NC)
    assert cpp%NC==0 and dl[4]%NC==0 and dl[8]%NC==0
    def copy_out_y(p): return pltpu.make_async_copy(outb.at[p],out_h.at[p],sem_out.at[0,p])
    def copy_out_x(p): return pltpu.make_async_copy(sgb.at[p],sg_h.at[p],sem_out.at[1,p])
    def copies_out(p): return copy_out_y(p),copy_out_x(p)
    dU[...]=jnp.zeros_like(dU); dN[...]=jnp.zeros_like(dN); dB[...]=jnp.zeros_like(dB)
    for r,q in zip(sizes,rings):
        n=min(r,dl[8]-dl[4]+4)
        q[pl.ds(r-n,n)]=jnp.zeros((n,64,L),BF)
    prologue(lay,recv,wu,wv,wd,wdb,pa,bias,dirs,cols)
    def slot(r,j): return j & (sizes[r]-1)
    def ld(r,j0,n):
        return jnp.concatenate([rings[r][slot(r,j0+k)] for k in range(n)],axis=1) if n>1 else rings[r][slot(r,j0)]
    def st(r,j0,v):
        v=v.astype(BF)
        for k in range(v.shape[1]//L): rings[r][slot(r,j0+k)]=v[:,k*L:(k+1)*L]
    def clampj(j): return min(max(j,0),NCOL-1) if isinstance(j,int) else jnp.clip(j,0,NCOL-1)
    def mult(x): return x if isinstance(x,int) else pl.multiple_of(x,NC*L)
    def cat0(*v): return jnp.concatenate(v,axis=0)
    def mask(kind,j0,rows,n):
        cols=[]
        for k in range(n):
            m=masks[clampj(j0+k),KINDS[kind]]
            cols.append(jnp.concatenate([m]*(rows//16),axis=0))
        return jnp.concatenate(cols,axis=1)
    def shf(x,k):
        W=x.shape[1]-2*L
        if k>0: return pltpu.roll(x[:,L:],W+L-k,1)[:,:W]
        return pltpu.roll(x[:,:W+L],-k,1)[:,L:]
    def stack(r,j0,n,b):
        x=ld(r,j0-1,n+2)
        E=x[:32]; O=x[32:]
        a_=(3**b-1)//2; b_=(3**b+1)//2
        Em=E[:,L:L+n*L]; Om=O[:,L:L+n*L]
        Omin=shf(O,-b_)*mask(-b_,j0,32,n)
        Opl=shf(O,a_)*mask(a_,j0,32,n) if a_ else Om
        Emin=shf(E,-a_)*mask(-a_,j0,32,n) if a_ else Em
        Epl=shf(E,b_)*mask(b_,j0,32,n)
        return jnp.concatenate([Omin,Em,Opl],axis=0),jnp.concatenate([Emin,Om,Epl],axis=0)
    def per_phase(w,xE,xO): return jnp.concatenate([dot(w,xE),dot(w,xO)],axis=0)
    def rowsum(v):
        s=v[:32]+v[32:]
        r=s[:,:L]
        for k in range(1,v.shape[1]//L): r=r+s[:,k*L:(k+1)*L]
        return r
    def biased(x,i):
        y=jnp.concatenate([bias[i]]*(x.shape[1]//L),axis=1)
        return x+jnp.concatenate([y,y],axis=0)
    def pc(j):
        jc=clampj(j)
        return (jc//cpp,jc%cpp) if isinstance(j,int) else (lax.div(jc,cpp),lax.rem(jc,cpp))
    def po(j):
        if isinstance(j,int): return pc(j)
        return jnp.where(j>=0,lax.div(clampj(j),cpp),packs), lax.rem(clampj(j),cpp)
    def stages(at, n):
        X={}
        jv=at[8]; jb=[at[7],at[6],at[5]]; jd=[at[2],at[3],at[4]]; ju=at[1]; jf=at[0]
        W=n*L
        def V1():
            x=ld(GU,jv-1,n+2)
            gt=cat0(x[:,L:L+W], shf(x[:32],1)*mask(1,jv,32,n), shf(x[32:],-1)*mask(-1,jv,32,n))
            y=dot(wv[...],gt)
            dU[:,:64]+=dot_nt(gt,ld(FIRST,jv,n))
            p,c=po(jv)
            sgb[p,:,pl.ds(mult(c*L),W)]=((0.2*y)*ld(DFIRST,jv,n).astype(F32)).astype(BF)
        def NT(b):
            g=ld(G[b],jb[b],n); act=ld(ACT[b],jb[b],n); hid=ld(HID[b],jb[b],n)
            dN[b,96:,:32]+=dot_nt(cat0(act[:32],hid[:32]),g[:32])+dot_nt(cat0(act[32:],hid[32:]),g[32:])
        def A(b):
            e,o=stack(GD[b],jb[b],n,b)
            g=ld(G[b],jb[b],n)
            X['A',b]=dot(wdb[b],cat0(e,g[:32])),dot(wdb[b],cat0(o,g[32:]))
            pre=ld(PRE[b],jb[b],n)
            dN[b,:96,:32]+=dot_nt(e,pre[:32])+dot_nt(o,pre[32:])
        def B2(b):
            x,y=X['A',b]
            gf=ld(DH[b],jb[b],n).astype(F32)*(0.2*cat0(x[:32],y[:32]))+cat0(x[32:],y[32:])
            gl=gf.astype(BF)
            if b==0:
                st(GU,jb[b],gl); dB[0,2]+=rowsum(gf)
            else:
                st(G[b-1],jb[b],gl); dB[b-1,1]+=rowsum(gf)
                X['g',b-1]=gl
        def AG(b):
            g=X['g',b]
            X['ag',b]=per_phase(pa[b,32:,64:],g[:32],g[32:])
        def PW(b):
            a=X['act',b]; h=ld(HID[b],jd[b],n)
            X['h',b]=per_phase(pa[b,:32,:64],cat0(a[:32],h[:32]),cat0(a[32:],h[32:]))
        def PA(b):
            a=X['act',b]; h=ld(HID[b],jd[b],n); g=X['g',b]
            x=dot(pa[b],cat0(a[:32],h[:32],g[:32])); y=dot(pa[b],cat0(a[32:],h[32:],g[32:]))
            X['h',b]=cat0(x[:32],y[:32]); X['ag',b]=cat0(x[32:],y[32:])
        def B3(b):
            gd=ld(DD[b-1],jb[b],n).astype(F32)*(0.2*X['ag',b-1])
            dB[b-1,0]+=rowsum(gd)
            st(GD[b-1],jb[b],gd)
        def D1(b):
            X['dil',b]=per_phase(wd[b],*stack(PRE[b],jd[b],n,b))
        def D2(b):
            act,dd=act_pair(biased(X['dil',b],1+2*b))
            act=act.astype(BF)
            st(ACT[b],jd[b],act)
            if b<2: st(DD[b],jd[b],dd)
            else: X['dd']=dd
            X['act',b]=act
        def G2f():
            p,c=pc(jd[2])
            gl=cot[p,:,pl.ds(mult(c*L),W)]
            st(G2,jd[2],gl)
            dB[2,1]+=rowsum(gl.astype(F32))
            X['g',2]=gl
        def D3(b):
            h=biased(X['h',b],2+2*b)
            if b<2:
                pre,dh=act_pair(h)
                st(PRE[b+1],jd[b],pre); st(HID[b+1],jd[b],h); st(DH[b+1],jd[b],dh)
            else:
                ho=h.astype(BF)
                z=cat0(*[jnp.concatenate([ho[:32,k*L:(k+1)*L],ho[32:,k*L:(k+1)*L]],axis=1) for k in range(n)])
                X['z']=dot(z,perm[...])
        def GD2f():
            gd=X['dd'].astype(F32)*(0.2*X['ag',2])
            dB[2,0]+=rowsum(gd)
            st(GD2,jd[2],gd)
        def O():
            z=X['z'].astype(BF)
            p,c=pc(jd[2])
            outb[p,:,pl.ds(mult(c*2*L),2*W)]=jnp.concatenate([z[k*32:(k+1)*32] for k in range(n)],axis=1)
        def U1():
            x=ld(FIRST,ju-1,n+2)
            fm=shf(x,-1)*mask(-1,ju,64,n); fp=shf(x,1)*mask(1,ju,64,n)
            X['u']=dot(wu[...],cat0(x[:,L:L+W],fm,fp))
        def U2():
            h=biased(X['u'],0)
            pre,dh=act_pair(h)
            st(PRE0,ju,pre); st(HID0,ju,h); st(DH0,ju,dh)
        def F():
            p,c=pc(jf if isinstance(jf,int) else jnp.minimum(jf,NCOL-n))
            fv,dv=act_pair(sig[p,:,pl.ds(mult(c*L),W)])
            st(FIRST,jf,fv); st(DFIRST,jf,dv)
        return {k: v for k,v in locals().items() if k in NAMES}
    def step(i):
        FULL(stages([i*NC-d for d in dl],NC))
    def chunks(first,end):
        return [(j,min(NC,end-j)) for j in range(first,end,NC)]
    def sweep(k,first,end,*calls):
        parts=[stages([j]*9,n) for j,n in chunks(first,end)]
        for call in calls:
            for e in parts: call(e)
    first=dl[4]//NC; last=first+NCOL//NC
    ipp=cpp//NC
    sweep(0,0,first*NC,lambda e: e["F"]())
    sweep(1,0,first*NC-dl[1],lambda e: e["U1"](),lambda e: e["U2"]())
    for b in range(2):
        sweep(2+b,0,first*NC-dl[2+b],lambda e: e["D1"](b),lambda e: e["D2"](b),lambda e: e["PW"](b),lambda e: e["D3"](b))
    done=-(-dl[8]//NC)+ipp
    assert (last-first)%UN==0
    def full(g,c):
        i=first+g*UN
        for k in range(UN):
            @pl.when((lax.rem(i-k,ipp)==done%ipp)&(i-k>=done))
            def _():
                for q in copies_out(lax.div(i-k-done,ipp)): q.start()
        for k in range(UN): step(i+k)
        return c
    lax.fori_loop(0,(last-first)//UN,full,0)
    begun=[first+g*UN-k for g in range((last-first)//UN) for k in range(UN)]
    started=[p for p in range(packs) if p*ipp+done in begun]
    out_left=range(len(started),packs)
    for p in out_left: copy_out_y(p).start()
    for b in (2,1):
        sweep(7-b,last*NC-dl[7-b],NCOL,lambda e: e["A"](b),lambda e: e["NT"](b),lambda e: e["B2"](b),lambda e: e["AG"](b-1),lambda e: e["B3"](b))
    sweep(7,last*NC-dl[7],NCOL,lambda e: e["A"](0),lambda e: e["NT"](0),lambda e: e["B2"](0))
    sweep(8,last*NC-dl[8],NCOL,lambda e: e["V1"]())
    for p in out_left: copy_out_x(p).start()
    for p in range(packs):
        for c in copies_out(p): c.wait()


def make_perm(perm, back=False):
    r=lax.broadcasted_iota(jnp.int32,(2*L,2*L),0); c=lax.broadcasted_iota(jnp.int32,(2*L,2*L),1)
    to=lambda x: jnp.where(x<L,2*x,2*(x-L)+1)
    perm[...]=((to(c)==r) if back else (to(r)==c)).astype(F32).astype(BF)


def main_call(NC, lay, signal, masks, cot, recv):
    packs,cin,T=signal.shape
    cpp=T//L
    V=pl.BlockSpec(memory_space=pltpu.VMEM); A=pl.BlockSpec(memory_space=pl.ANY)
    return pl.pallas_call(
        functools.partial(main_kernel,NC,packs,cpp,lay),
        name="section",
        out_shape=(jax.ShapeDtypeStruct((packs,32,2*T),BF),jax.ShapeDtypeStruct(signal.shape,BF),
            *[jax.ShapeDtypeStruct(x,F32) for x in ((L,L),(3,160,L),(3,3,32,L),(256,L),(2,256,L))]),
        in_specs=[V]*4, out_specs=(A,A,V,V,V,V,V),
        scratch_shapes=[pltpu.VMEM((packs,32,2*T),BF),pltpu.VMEM((packs+1,64,T),BF),
            pltpu.VMEM((7,32,L),F32),
            pltpu.SemaphoreType.DMA((2,packs))],
        compiler_params=pltpu.CompilerParams(vmem_limit_bytes=VMEM<<20),
    )(signal,masks,cot,recv)

from jax.sharding import PartitionSpec as P

MESH = pl.DeviceIdType.MESH


def peer(lay, k):
    me = lax.axis_index("dp") * lay.nf + lax.axis_index("fsdp")
    t = lax.rem(me + k, lay.n)
    return me, t, {"dp": t // lay.nf, "fsdp": lax.rem(t, lay.nf)}


def greet(lay):
    barrier = pltpu.get_barrier_semaphore()

    def hello(k, c):
        _, _, dev = peer(lay, k)
        pl.semaphore_signal(barrier, inc=1, device_id=dev, device_id_type=MESH)
        return c

    lax.fori_loop(1, lay.n, hello, 0)
    return barrier


def copy_out(lay, source, recv, send_sem, recv_sem, k):
    me, t, dev = peer(lay, k)
    return pltpu.make_async_remote_copy(
        src_ref=source(t), dst_ref=recv.at[me], send_sem=send_sem.at[k], recv_sem=recv_sem.at[k],
        device_id=dev, device_id_type=MESH)


def send(lay, *args):
    def start(k, c):
        copy_out(lay, *args, k).start()
        return c

    lax.fori_loop(1, lay.n, start, 0)


def receive(lay, *args):
    def finish(k, c):
        copy_out(lay, *args, k).wait()
        return c

    lax.fori_loop(1, lay.n, finish, 0)


def gather_kernel(lay, cot_h, *refs):
    shards_h, seg_h, (out, split, masks), shards = refs[:7], refs[7], refs[8:11], refs[11:18]
    acc, sq, msg, recv, perm, cot, seg, send_sem, recv_sem, in_sem, seg_sem, shard_sem = refs[18:]
    packs, _, width = cot_h.shape
    load = [pltpu.make_async_copy(h, v, shard_sem.at[k]) for k, (h, v) in enumerate(zip(shards_h, shards)) if v.size > 1]
    shards = [h if h.size == 1 else v for h, v in zip(shards_h, shards)]
    fetch = [pltpu.make_async_copy(cot_h.at[p], cot.at[p], in_sem.at[p]) for p in range(packs)]
    barrier = greet(lay)
    count = pltpu.make_async_copy(seg_h, seg, seg_sem)
    for c in load + [count] + fetch:
        c.start()
    acc[...] = jnp.zeros_like(acc)
    sq[...] = jnp.zeros_like(sq)
    for c in load:
        c.wait()
    ud, dd, pd, ug, ub, rg, rb = shards
    for p, o in enumerate(lay.u):
        acc[:, o:o + lay.wu] = ud[8 * p:8 * p + 8].astype(F32)
    for b in range(3):
        acc[:, lay.d[b]:lay.d[b] + lay.wd] = dd[b].astype(F32)
        for j in range(2):
            o = (2 * b + j) * lay.wp
            sq[o:o + lay.wp, 0:8] = pd[b, j].astype(F32)
        o = lay.r[b]
        acc[0:3, o:o + lay.wr] = rg[b].astype(F32)
        acc[3:6, o:o + lay.wr] = rb[b].astype(F32)
    acc[0:1, lay.g:lay.g + lay.wg] = ug[...].astype(F32)
    acc[1:2, lay.g:lay.g + lay.wr] = ub[...].astype(F32)
    full = put(acc[...], sq[...].T[:8], 0, lay.p[0], 6 * lay.wp).astype(BF)
    msg[...] = full
    me = peer(lay, 0)[0]
    recv[me] = full
    step = 8

    def part(p):
        fetch[p].wait()
        for k in range(0, width // (2 * L), step):
            x = jnp.concatenate([cot[p, :, (k + q) * 2 * L:(k + q + 1) * 2 * L] for q in range(step)], axis=0)
            z = dot(x, perm[...]).astype(BF)
            for e in range(2):
                y = jnp.concatenate([z[q * 32:(q + 1) * 32, e * L:(e + 1) * L] for q in range(step)], axis=1)
                split[p, e * 32:(e + 1) * 32, k * L:(k + step) * L] = y

    pl.semaphore_wait(barrier, lay.n - 1)
    args = (lambda t: msg, recv, send_sem, recv_sem)
    send(lay, *args)
    count.wait()
    make_masks(seg, masks, width // (2 * L))
    make_perm(perm, True)
    for p in range(packs):
        part(p)
    receive(lay, *args)
    out[...] = recv[...]


def scatter_kernel(lay, dU, dN, dB, dirs, cols, out, tmp, msgs, recv, send_sem, recv_sem):
    barrier = greet(lay)
    epilogue(lay, dU, dN, dB, dirs, cols, tmp, msgs)
    me = peer(lay, 0)[0]
    recv[me] = msgs[me]
    pl.semaphore_wait(barrier, lay.n - 1)
    args = (lambda t: msgs.at[t], recv, send_sem, recv_sem)
    send(lay, *args)
    receive(lay, *args)
    out[...] = recv[...]


def sum_kernel(lay, recv, gud, gug, gub, gdd, gpd, grg, grb):
    t = recv[0].astype(F32)
    for s in range(1, lay.n):
        t = t + recv[s].astype(F32)
    m = jnp.concatenate([move(t, lay.p[0], 0), jnp.zeros((L - 8, L), F32)], axis=0).T
    for p, o in enumerate(lay.u):
        gud[8 * p:8 * p + 8] = t[:, o:o + lay.wu]
    for b in range(3):
        gdd[b] = t[:, lay.d[b]:lay.d[b] + lay.wd]
        for j in range(2):
            o = (2 * b + j) * lay.wp
            gpd[b, j] = m[o:o + lay.wp, 0:8]
        o = lay.r[b]
        grg[b] = t[0:3, o:o + lay.wr]
        grb[b] = t[3:6, o:o + lay.wr]
    gug[...] = t[0:1, lay.g:lay.g + lay.wg]
    gub[...] = t[1:2, lay.g:lay.g + lay.wr]


def per_device(lay, signal, segments, cotangent, ud, ug, ub, dd, pd, rg, rb):
    V = pl.BlockSpec(memory_space=pltpu.VMEM)
    tiles = jax.ShapeDtypeStruct((lay.n, 8, L), BF)
    sems = [pltpu.SemaphoreType.DMA((lay.n,)), pltpu.SemaphoreType.DMA((lay.n,))]
    packs, _, width = cotangent.shape
    parted = (packs, 64, width // 2)
    H = pl.BlockSpec(memory_space=pltpu.HBM)
    shards = (ud, dd, pd.transpose(0, 1, 3, 2), ug.reshape(1, -1), ub.reshape(1, -1), rg, rb)
    table, split, masks = pl.pallas_call(
        functools.partial(gather_kernel, lay), name="gather_params", out_shape=(tiles, jax.ShapeDtypeStruct(parted, BF), jax.ShapeDtypeStruct((packs * width // (2 * L), 8, 16, L), BF)),
        in_specs=[H] + [H if v.size > 1 else V for v in shards] + [H], out_specs=(V, V, V),
        scratch_shapes=[pltpu.VMEM(v.shape, v.dtype) for v in shards] + [pltpu.VMEM((8, L), F32), pltpu.VMEM((L, L), F32), pltpu.VMEM((8, L), BF), pltpu.VMEM((lay.n, 8, L), BF),
                        pltpu.VMEM((2 * L, 2 * L), BF), pltpu.VMEM(cotangent.shape, BF), pltpu.VMEM(segments.shape, jnp.int32)] + sems
        + [pltpu.SemaphoreType.DMA((packs,)), pltpu.SemaphoreType.DMA, pltpu.SemaphoreType.DMA((7,))],
        compiler_params=pltpu.CompilerParams(collective_id=0, has_side_effects=True, vmem_limit_bytes=20 << 20),
    )(*(pltpu.with_memory_space_constraint(v, pltpu.HBM) if v.size > 1 else v for v in (cotangent, *shards, segments)))
    out, sg, *sums = main_call(NC, lay, signal, masks, split, table)
    got = pl.pallas_call(
        functools.partial(scatter_kernel, lay), name="scatter_grads", out_shape=tiles,
        in_specs=[V] * 5, out_specs=V,
        scratch_shapes=[pltpu.VMEM((6, 32, L), F32), pltpu.VMEM((lay.n, 8, L), BF), pltpu.VMEM((lay.n, 8, L), BF)] + sems,
        compiler_params=pltpu.CompilerParams(collective_id=1, has_side_effects=True, vmem_limit_bytes=4 << 20),
    )(*sums)
    f = lambda *s: jax.ShapeDtypeStruct(s, F32)
    gud, gug, gub, gdd, gpd, grg, grb = pl.pallas_call(
        functools.partial(sum_kernel, lay), name="sum_grads",
        out_shape=(f(*ud.shape), f(1, ug.shape[0]), f(1, ub.shape[0]), f(*dd.shape), f(3, 2, pd.shape[3], pd.shape[2]), f(*rg.shape), f(*rb.shape)),
        in_specs=[V], out_specs=(V,) * 7,
        compiler_params=pltpu.CompilerParams(vmem_limit_bytes=2 << 20),
    )(got)
    return out, sg, gud, gug.reshape(-1), gub.reshape(-1), gdd, gpd.transpose(0, 1, 3, 2), grg, grb


NC = 4


def solution(mesh):
    lay = Lay(mesh.shape["dp"], mesh.shape["fsdp"])
    return jax.shard_map(
        functools.partial(per_device, lay),
        mesh=mesh,
        in_specs=(
            P(("dp", "fsdp"), None, None),
            P(("dp", "fsdp"), None),
            P(("dp", "fsdp"), None, None),
            P("dp", "fsdp"),
            P("fsdp"),
            P("fsdp"),
            P(None, "dp", "fsdp"),
            P(None, None, "dp", "fsdp"),
            P(None, None, "fsdp"),
            P(None, None, "fsdp"),
        ),
        out_specs=(
            P(("dp", "fsdp"), None, None),
            P(("dp", "fsdp"), None, None),
            P("dp", "fsdp"),
            P("fsdp"),
            P("fsdp"),
            P(None, "dp", "fsdp"),
            P(None, None, "dp", "fsdp"),
            P(None, None, "fsdp"),
            P(None, None, "fsdp"),
        ),
        check_vma=False,
    )
```

```python
import functools
import jax, jax.numpy as jnp
from jax import lax
from jax.experimental import pallas as pl
from jax.experimental.pallas import tpu as pltpu

BF=jnp.bfloat16; F32=jnp.float32
L=128

def dot(a,b):
    return jnp.dot(a,b,preferred_element_type=F32)
def dot_nt(a,b):
    return lax.dot_general(a,b,(((1,),(1,)),((),())),preferred_element_type=F32)

def act_pair(h):
    h=h.astype(F32)
    v=h.astype(BF); w=(0.2*h).astype(BF)
    c=lambda x: jnp.asarray(x,BF)
    th=jnp.tanh(c(0.5)*v); t=c(3.0)+c(2.0)*th; q=c(1.0)-th*th
    return w*t, t+v*q

KINDS={-1:0,1:1,-2:2,2:3,-4:4,4:5,-5:6,5:7}

NAMES=("V1","NT","A","B2","AG","PW","PA","B3","D1","D2","G2f","D3","GD2f","O","U1","U2","F")


def FULL(e):
    V1,NT,A,B2,AG,PW,PA,B3,D1,D2,G2f,D3,GD2f,O,U1,U2,F=[e[k] for k in NAMES]
    G2f(); D1(2); NT(2); A(2); D2(2); D1(1); NT(1); D1(0)
    PA(2); A(1); V1(); D2(1); B2(2); PA(1); B3(2); GD2f()
    B2(1); D2(0); D3(2); F(); A(0); PA(0); U1(); D3(1)
    O(); NT(0); B3(1); D3(0); B2(0); U2()


def lags(NC):
    out=[0]
    for k in range(8):
        d=out[-1]+NC+1
        out.append(-(-d//NC)*NC if k in (3,7) else d)
    return out


def ring_sizes(NC):
    F,U,D0,D1,D2,B2,B1,B0,V=range(9)
    life=[(F,V),(F,V),(U,B0),(D0,B1),(D1,B2),(U,B0),(D0,B1),(D1,B2),(U,B0),(D0,B1),(D1,B2),
          (D0,B0),(D1,B1),(D2,B2),(D0,B1),(D1,B2),(D2,B2),(B2,B1),(B1,B0),(B1,B0),(B2,B1),(D2,B2),(D2,V)]
    out=[]; lag=lags(NC)
    for w,r in life:
        need=lag[r]-lag[w]+NC+2
        out.append(max(8,1<<(need-1).bit_length()))
    return out


UN=8
VMEM=28


class Lay:
    def __init__(self, nd, nf):
        self.nd, self.nf, self.n = nd, nf, nd * nf
        self.wu, self.wd, self.wp, self.wr, self.wg = 128 // nf, 96 // nf, 32 // nf, 32 // nf, 64 // nf
        self.pu = 64 // nd // 8
        at = 0
        self.u = []
        for _ in range(self.pu):
            self.u.append(at)
            at += self.wu
        self.d = []
        for _ in range(3):
            self.d.append(at)
            at += self.wd
        self.p = []
        for _ in range(6):
            self.p.append(at)
            at += self.wp
        self.r = []
        for _ in range(3):
            self.r.append(at)
            at += self.wr
        self.g = at
        assert at + self.wg <= 128


def lane8(): return lax.broadcasted_iota(jnp.int32,(8,L),1)


def move(x, frm, to):
    k=(to-frm)%L
    return x if k==0 else pltpu.roll(x,k,1)


def put(acc, x, frm, to, w):
    lane=lane8()
    return jnp.where((lane>=to)&(lane<to+w),move(x,frm,to),acc)


def tap_perm():
    r=lax.broadcasted_iota(jnp.int32,(L,L),0); c=lax.broadcasted_iota(jnp.int32,(L,L),1)
    pos=((r&3)+3)&3
    return (c==pos*32+(r>>2)).astype(F32).astype(BF)


def square(x):
    return jnp.concatenate([x,jnp.zeros((L-x.shape[0],L),F32)],axis=0) if x.shape[0]<L else x


def prologue(lay, recv, wu, wv, wd, wdb, pa, bias, dirs, cols):
    nd,nf=lay.nd,lay.nf
    z=jnp.zeros((8,L),F32)
    lane=lane8()
    def pick(x, at, w, acc):
        at=at%L
        return jnp.where((lane>=at)&(lane<at+w),x,acc)
    def gather(i, o, w, count):
        acc=[z]*count
        for f in range(nf):
            x=move(recv[i*nf+f].astype(F32),o,f*w)
            acc=[pick(x,(f+q)*w,w,y) for q,y in enumerate(acc)]
        return acc
    ud=jnp.concatenate([move(x,p*lay.wu,0) for i in range(nd) for p,x in enumerate(gather(i,lay.u[0],lay.wu,lay.pu))],axis=0)
    dd=[[] for _ in range(3)]; pd=[[] for _ in range(3)]
    for i in range(nd):
        x=gather(i,lay.d[0],lay.wd,3); y=gather(i,lay.p[0],lay.wp,6)
        for b in range(3):
            dd[b].append(move(x[b],b*lay.wd,0))
            pd[b].append(move(y[2*b],2*b*lay.wp,0)+move(y[2*b+1],(2*b+1)*lay.wp,32))
    dd=[jnp.concatenate(x,axis=0) for x in dd]; pd=[jnp.concatenate(x,axis=0) for x in pd]
    sm=[move(x,b*lay.wr,0) for b,x in enumerate(gather(0,lay.r[0],lay.wr,3))]+gather(0,lay.g,lay.wg,1)+gather(0,lay.g,lay.wr,1)
    st=square(jnp.concatenate(sm,axis=0)).T
    def col(q,rows): return jnp.broadcast_to(st[:rows,q:q+1],(rows,L))
    def norm(x): return jnp.broadcast_to(jnp.sqrt(jnp.sum(x*x,axis=1,keepdims=True)),x.shape)
    n=norm(ud); g=col(24,64)
    dirs[0:64]=ud; cols[0,0:64]=g/n; cols[1,0:64]=1.0/n
    w=dot((g*ud/n).astype(BF),tap_perm())
    wv[...]=w.astype(BF)
    m=jnp.concatenate([w,pltpu.roll(w,64,1)],axis=0).T
    lane=lax.broadcasted_iota(jnp.int32,(32,L),1)
    z32=jnp.zeros((32,L),F32)
    def left(x): return jnp.where(lane<64,x,0.0)
    x=jnp.concatenate([jnp.concatenate([m[:32],z32],axis=1),
                       jnp.concatenate([left(m[32:64]),left(pltpu.roll(m[32:64],64,1))],axis=1)],axis=0)
    wu[...]=x[:,:192].astype(BF)
    bias[0]=col(33,32)
    for b in range(3):
        r=64+32*b
        x=dd[b]; n=norm(x); g=col(8*b,32)
        dirs[r:r+32]=x; cols[0,r:r+32]=g/n; cols[1,r:r+32]=1.0/n
        w=(g*x/n).astype(BF).astype(F32)
        wd[b]=w[:,:96].astype(BF)
        m=square(jnp.concatenate([pltpu.roll(w,64,1),pltpu.roll(w,96,1),w],axis=0)).T
        back=m[:32]
        r=160+32*b
        x=pd[b]
        n=jnp.where(lane<32,norm(jnp.where(lane<32,x,0.0)),norm(jnp.where(lane<32,0.0,x)))
        g=jnp.where(lane<32,col(8*b+1,32),col(8*b+2,32))
        dirs[r:r+32]=x; cols[0,r:r+32]=g/n; cols[1,r:r+32]=1.0/n
        w=(g*x/n).astype(BF)
        w=w.astype(F32)
        m=square(w).T
        wide=jnp.where(lane<32,m[:64][32:],0.0)
        wdb[b]=jnp.concatenate([back,pltpu.roll(wide,96,1)],axis=0).astype(BF)
        wide=jnp.where(lane<32,m[:32],0.0)
        pa[b]=jnp.concatenate([w,pltpu.roll(wide,64,1)],axis=0)[:,:96].astype(BF)
        bias[1+2*b]=col(8*b+3,32)
        bias[2+2*b]=col(8*b+4,32)+col(8*b+5,32)


def epilogue(lay, dU, dN, dB, dirs, cols, tmp, msgs):
    nd,nf=lay.nd,lay.nf
    def rs(x): return jnp.sum(x,axis=1,keepdims=True)
    lane=lax.broadcasted_iota(jnp.int32,(64,L),1); lane32=lane[:32]
    C=jnp.zeros((64,L),F32)
    def place(C,q,c):
        c=jnp.broadcast_to(c,(c.shape[0],L))
        if c.shape[0]==32: c=jnp.concatenate([c,jnp.zeros((32,L),F32)],axis=0)
        return jnp.where(lane==q,c,C)
    perm=tap_perm()
    v=dot(dirs[0:64].astype(BF),perm); w=dU[...].T[:64]; s=cols[0,0:64]; i=cols[1,0:64]
    inner=rs(w*v)
    C=place(C,24,inner*i)
    g=s*(w-(inner*i*i)*v)
    gu=dot_nt(g.astype(BF),perm)
    gd=[];gp=[]
    tmp[...]=jnp.zeros_like(tmp)
    for b in range(3):
        r=64+32*b
        for t in range(3): tmp[b,:,t*32:t*32+32]=dN[b,(2-t)*32:(3-t)*32,:32]
        v=dirs[r:r+32]; w=tmp[b]; s=cols[0,r:r+32]; i=cols[1,r:r+32]
        inner=rs(w*v)
        C=place(C,8*b,inner*i)
        gd.append(s*(w-(inner*i*i)*v))
        r=160+32*b
        tmp[3+b]=square(dN[b,96:160]).T[:32]
        v=dirs[r:r+32]; w=tmp[3+b]; s=cols[0,r:r+32]; i=cols[1,r:r+32]
        p=w*v
        inner=jnp.where(lane32<32,rs(jnp.where(lane32<32,p,0.0)),rs(jnp.where(lane32<32,0.0,p)))
        C=place(C,8*b+1,inner[:,:1]*i[:,:1])
        C=place(C,8*b+2,inner[:,32:33]*i[:,32:33])
        gp.append(s*(w-(inner*i*i)*v))
        C=place(C,8*b+3,rs(dB[b,0]))
        o=rs(dB[b,1])
        C=place(C,8*b+4,o); C=place(C,8*b+5,o)
    C=place(C,33,rs(dB[0,2]))
    S=square(C).T
    lane=lane8(); row=lax.broadcasted_iota(jnp.int32,(8,L),0)
    def join(xs, f, w, o):
        acc=xs[0]
        for q,x in enumerate(xs[1:],1):
            at=(f+q)*w%L
            acc=jnp.where((lane>=at)&(lane<at+w),x,acc)
        return move(acc,f*w,o)
    def upto(at, x, y): return jnp.where(lane<at,x,y)
    us=[[move(gu[(d*lay.pu+p)*8:(d*lay.pu+p)*8+8],0,p*lay.wu) for p in range(lay.pu)] for d in range(nd)]
    ds=[[move(gd[b][8*d:8*d+8],0,b*lay.wd) for b in range(3)] for d in range(nd)]
    ps=[[move(gp[q//2][8*d:8*d+8],32*(q%2),q*lay.wp) for q in range(6)] for d in range(nd)]
    rs_=[move(S[8*b:8*b+8],0,b*lay.wr) for b in range(3)]
    for f in range(nf):
        g=jnp.where(row==1,move(S[32:40],f*lay.wr,lay.g),move(S[24:32],f*lay.wg,lay.g))
        sm=upto(lay.g,join(rs_,f,lay.wr,lay.r[0]),jnp.where(lane<lay.g+lay.wg,g,0.0))
        for d in range(nd):
            x=upto(lay.d[0],join(us[d],f,lay.wu,lay.u[0]),
              upto(lay.p[0],join(ds[d],f,lay.wd,lay.d[0]),
              upto(lay.r[0],join(ps[d],f,lay.wp,lay.p[0]),sm)))
            msgs[d*nf+f]=x.astype(BF)


def make_masks(seg, masks, cpp):
    T=cpp*L
    s=seg[...]
    pos=lax.broadcasted_iota(jnp.int32,s.shape,1)
    for k,kind in KINDS.items():
        r=pltpu.roll(s,(-k)%T,1)
        m=((r==s)&(pos+k>=0)&(pos+k<T)).astype(F32)
        for p in range(s.shape[0]):
            mp=jnp.broadcast_to(m[p:p+1,:],(16,T)).astype(BF)
            for c in range(cpp): masks[p*cpp+c,kind]=mp[:,c*L:(c+1)*L]


def main_kernel(NC, packs, cpp, lay, sig, masks, cot, recv, out_h, sg_h, dU, dN, dB, dirs, cols,
                outb, sgb, bias, sem_out):
    def body(wu, wv, wd, wdb, pa, perm, *rings):
        make_perm(perm)
        main_body(NC,packs,cpp,lay,recv,wu,wv,wd,wdb,pa,bias,perm,out_h,sg_h,dU,dN,dB,
                  sig,cot,outb,sgb,dirs,cols,sem_out,masks,rings)
    pl.run_scoped(body,pltpu.VMEM((64,192),BF),pltpu.VMEM((64,L),BF),pltpu.VMEM((3,32,96),BF),pltpu.VMEM((3,64,L),BF),
                  pltpu.VMEM((3,64,96),BF),pltpu.VMEM((2*L,2*L),BF),
                  *[pltpu.VMEM((r,64,L),BF) for r in ring_sizes(NC)])


def main_body(NC, packs, cpp, lay, recv, wu, wv, wd, wdb, pa, bias, perm,
              out_h, sg_h, dU, dN, dB, sig, cot, outb, sgb, dirs, cols, sem_out, masks, rings):
    NCOL=packs*cpp
    (FIRST,DFIRST,PRE0,PRE1,PRE2,HID0,HID1,HID2,DH0,DH1,DH2,ACT0,ACT1,ACT2,DD0,DD1,G2,G1,G0,GD0,GD1,GD2,GU)=range(23)
    PRE=(PRE0,PRE1,PRE2);HID=(HID0,HID1,HID2);DH=(DH0,DH1,DH2);ACT=(ACT0,ACT1,ACT2);DD=(DD0,DD1);GD=(GD0,GD1,GD2);G=(G0,G1,G2)
    dl=lags(NC)
    sizes=ring_sizes(NC)
    assert cpp%NC==0 and dl[4]%NC==0 and dl[8]%NC==0
    def copy_out_y(p): return pltpu.make_async_copy(outb.at[p],out_h.at[p],sem_out.at[0,p])
    def copy_out_x(p): return pltpu.make_async_copy(sgb.at[p],sg_h.at[p],sem_out.at[1,p])
    def copies_out(p): return copy_out_y(p),copy_out_x(p)
    dU[...]=jnp.zeros_like(dU); dN[...]=jnp.zeros_like(dN); dB[...]=jnp.zeros_like(dB)
    for r,q in zip(sizes,rings):
        n=min(r,dl[8]-dl[4]+4)
        q[pl.ds(r-n,n)]=jnp.zeros((n,64,L),BF)
    prologue(lay,recv,wu,wv,wd,wdb,pa,bias,dirs,cols)
    def slot(r,j): return j & (sizes[r]-1)
    def ld(r,j0,n):
        return jnp.concatenate([rings[r][slot(r,j0+k)] for k in range(n)],axis=1) if n>1 else rings[r][slot(r,j0)]
    def st(r,j0,v):
        v=v.astype(BF)
        for k in range(v.shape[1]//L): rings[r][slot(r,j0+k)]=v[:,k*L:(k+1)*L]
    def clampj(j): return min(max(j,0),NCOL-1) if isinstance(j,int) else jnp.clip(j,0,NCOL-1)
    def mult(x): return x if isinstance(x,int) else pl.multiple_of(x,NC*L)
    def cat0(*v): return jnp.concatenate(v,axis=0)
    def mask(kind,j0,rows,n):
        cols=[]
        for k in range(n):
            m=masks[clampj(j0+k),KINDS[kind]]
            cols.append(jnp.concatenate([m]*(rows//16),axis=0))
        return jnp.concatenate(cols,axis=1)
    def shf(x,k):
        W=x.shape[1]-2*L
        if k>0: return pltpu.roll(x[:,L:],W+L-k,1)[:,:W]
        return pltpu.roll(x[:,:W+L],-k,1)[:,L:]
    def stack(r,j0,n,b):
        x=ld(r,j0-1,n+2)
        E=x[:32]; O=x[32:]
        a_=(3**b-1)//2; b_=(3**b+1)//2
        Em=E[:,L:L+n*L]; Om=O[:,L:L+n*L]
        Omin=shf(O,-b_)*mask(-b_,j0,32,n)
        Opl=shf(O,a_)*mask(a_,j0,32,n) if a_ else Om
        Emin=shf(E,-a_)*mask(-a_,j0,32,n) if a_ else Em
        Epl=shf(E,b_)*mask(b_,j0,32,n)
        return jnp.concatenate([Omin,Em,Opl],axis=0),jnp.concatenate([Emin,Om,Epl],axis=0)
    def per_phase(w,xE,xO): return jnp.concatenate([dot(w,xE),dot(w,xO)],axis=0)
    def rowsum(v):
        s=v[:32]+v[32:]
        r=s[:,:L]
        for k in range(1,v.shape[1]//L): r=r+s[:,k*L:(k+1)*L]
        return r
    def biased(x,i):
        y=jnp.concatenate([bias[i]]*(x.shape[1]//L),axis=1)
        return x+jnp.concatenate([y,y],axis=0)
    def pc(j):
        jc=clampj(j)
        return (jc//cpp,jc%cpp) if isinstance(j,int) else (lax.div(jc,cpp),lax.rem(jc,cpp))
    def po(j):
        if isinstance(j,int): return pc(j)
        return jnp.where(j>=0,lax.div(clampj(j),cpp),packs), lax.rem(clampj(j),cpp)
    def stages(at, n):
        X={}
        jv=at[8]; jb=[at[7],at[6],at[5]]; jd=[at[2],at[3],at[4]]; ju=at[1]; jf=at[0]
        W=n*L
        def V1():
            x=ld(GU,jv-1,n+2)
            gt=cat0(x[:,L:L+W], shf(x[:32],1)*mask(1,jv,32,n), shf(x[32:],-1)*mask(-1,jv,32,n))
            y=dot(wv[...],gt)
            dU[:,:64]+=dot_nt(gt,ld(FIRST,jv,n))
            p,c=po(jv)
            sgb[p,:,pl.ds(mult(c*L),W)]=((0.2*y)*ld(DFIRST,jv,n).astype(F32)).astype(BF)
        def NT(b):
            g=ld(G[b],jb[b],n); act=ld(ACT[b],jb[b],n); hid=ld(HID[b],jb[b],n)
            dN[b,96:,:32]+=dot_nt(cat0(act[:32],hid[:32]),g[:32])+dot_nt(cat0(act[32:],hid[32:]),g[32:])
        def A(b):
            e,o=stack(GD[b],jb[b],n,b)
            g=ld(G[b],jb[b],n)
            X['A',b]=dot(wdb[b],cat0(e,g[:32])),dot(wdb[b],cat0(o,g[32:]))
            pre=ld(PRE[b],jb[b],n)
            dN[b,:96,:32]+=dot_nt(e,pre[:32])+dot_nt(o,pre[32:])
        def B2(b):
            x,y=X['A',b]
            gf=ld(DH[b],jb[b],n).astype(F32)*(0.2*cat0(x[:32],y[:32]))+cat0(x[32:],y[32:])
            gl=gf.astype(BF)
            if b==0:
                st(GU,jb[b],gl); dB[0,2]+=rowsum(gf)
            else:
                st(G[b-1],jb[b],gl); dB[b-1,1]+=rowsum(gf)
                X['g',b-1]=gl
        def AG(b):
            g=X['g',b]
            X['ag',b]=per_phase(pa[b,32:,64:],g[:32],g[32:])
        def PW(b):
            a=X['act',b]; h=ld(HID[b],jd[b],n)
            X['h',b]=per_phase(pa[b,:32,:64],cat0(a[:32],h[:32]),cat0(a[32:],h[32:]))
        def PA(b):
            a=X['act',b]; h=ld(HID[b],jd[b],n); g=X['g',b]
            x=dot(pa[b],cat0(a[:32],h[:32],g[:32])); y=dot(pa[b],cat0(a[32:],h[32:],g[32:]))
            X['h',b]=cat0(x[:32],y[:32]); X['ag',b]=cat0(x[32:],y[32:])
        def B3(b):
            gd=ld(DD[b-1],jb[b],n).astype(F32)*(0.2*X['ag',b-1])
            dB[b-1,0]+=rowsum(gd)
            st(GD[b-1],jb[b],gd)
        def D1(b):
            X['dil',b]=per_phase(wd[b],*stack(PRE[b],jd[b],n,b))
        def D2(b):
            act,dd=act_pair(biased(X['dil',b],1+2*b))
            act=act.astype(BF)
            st(ACT[b],jd[b],act)
            if b<2: st(DD[b],jd[b],dd)
            else: X['dd']=dd
            X['act',b]=act
        def G2f():
            p,c=pc(jd[2])
            gl=cot[p,:,pl.ds(mult(c*L),W)]
            st(G2,jd[2],gl)
            dB[2,1]+=rowsum(gl.astype(F32))
            X['g',2]=gl
        def D3(b):
            h=biased(X['h',b],2+2*b)
            if b<2:
                pre,dh=act_pair(h)
                st(PRE[b+1],jd[b],pre); st(HID[b+1],jd[b],h); st(DH[b+1],jd[b],dh)
            else:
                ho=h.astype(BF)
                z=cat0(*[jnp.concatenate([ho[:32,k*L:(k+1)*L],ho[32:,k*L:(k+1)*L]],axis=1) for k in range(n)])
                X['z']=dot(z,perm[...])
        def GD2f():
            gd=X['dd'].astype(F32)*(0.2*X['ag',2])
            dB[2,0]+=rowsum(gd)
            st(GD2,jd[2],gd)
        def O():
            z=X['z'].astype(BF)
            p,c=pc(jd[2])
            outb[p,:,pl.ds(mult(c*2*L),2*W)]=jnp.concatenate([z[k*32:(k+1)*32] for k in range(n)],axis=1)
        def U1():
            x=ld(FIRST,ju-1,n+2)
            fm=shf(x,-1)*mask(-1,ju,64,n); fp=shf(x,1)*mask(1,ju,64,n)
            X['u']=dot(wu[...],cat0(x[:,L:L+W],fm,fp))
        def U2():
            h=biased(X['u'],0)
            pre,dh=act_pair(h)
            st(PRE0,ju,pre); st(HID0,ju,h); st(DH0,ju,dh)
        def F():
            p,c=pc(jf if isinstance(jf,int) else jnp.minimum(jf,NCOL-n))
            fv,dv=act_pair(sig[p,:,pl.ds(mult(c*L),W)])
            st(FIRST,jf,fv); st(DFIRST,jf,dv)
        return {k: v for k,v in locals().items() if k in NAMES}
    def step(i):
        FULL(stages([i*NC-d for d in dl],NC))
    def chunks(first,end):
        return [(j,min(NC,end-j)) for j in range(first,end,NC)]
    def sweep(k,first,end,*calls):
        parts=[stages([j]*9,n) for j,n in chunks(first,end)]
        for call in calls:
            for e in parts: call(e)
    first=dl[4]//NC; last=first+NCOL//NC
    ipp=cpp//NC
    sweep(0,0,first*NC,lambda e: e["F"]())
    sweep(1,0,first*NC-dl[1],lambda e: e["U1"](),lambda e: e["U2"]())
    for b in range(2):
        sweep(2+b,0,first*NC-dl[2+b],lambda e: e["D1"](b),lambda e: e["D2"](b),lambda e: e["PW"](b),lambda e: e["D3"](b))
    done=-(-dl[8]//NC)+ipp
    assert (last-first)%UN==0
    def full(g,c):
        i=first+g*UN
        for k in range(UN):
            @pl.when((lax.rem(i-k,ipp)==done%ipp)&(i-k>=done))
            def _():
                for q in copies_out(lax.div(i-k-done,ipp)): q.start()
        for k in range(UN): step(i+k)
        return c
    lax.fori_loop(0,(last-first)//UN,full,0)
    begun=[first+g*UN-k for g in range((last-first)//UN) for k in range(UN)]
    started=[p for p in range(packs) if p*ipp+done in begun]
    out_left=range(len(started),packs)
    for p in out_left: copy_out_y(p).start()
    for b in (2,1):
        sweep(7-b,last*NC-dl[7-b],NCOL,lambda e: e["A"](b),lambda e: e["NT"](b),lambda e: e["B2"](b),lambda e: e["AG"](b-1),lambda e: e["B3"](b))
    sweep(7,last*NC-dl[7],NCOL,lambda e: e["A"](0),lambda e: e["NT"](0),lambda e: e["B2"](0))
    sweep(8,last*NC-dl[8],NCOL,lambda e: e["V1"]())
    for p in out_left: copy_out_x(p).start()
    for p in range(packs):
        for c in copies_out(p): c.wait()


def make_perm(perm, back=False):
    r=lax.broadcasted_iota(jnp.int32,(2*L,2*L),0); c=lax.broadcasted_iota(jnp.int32,(2*L,2*L),1)
    to=lambda x: jnp.where(x<L,2*x,2*(x-L)+1)
    perm[...]=((to(c)==r) if back else (to(r)==c)).astype(F32).astype(BF)


def main_call(NC, lay, signal, masks, cot, recv):
    packs,cin,T=signal.shape
    cpp=T//L
    V=pl.BlockSpec(memory_space=pltpu.VMEM); A=pl.BlockSpec(memory_space=pl.ANY)
    return pl.pallas_call(
        functools.partial(main_kernel,NC,packs,cpp,lay),
        name="section",
        out_shape=(jax.ShapeDtypeStruct((packs,32,2*T),BF),jax.ShapeDtypeStruct(signal.shape,BF),
            *[jax.ShapeDtypeStruct(x,F32) for x in ((L,L),(3,160,L),(3,3,32,L),(256,L),(2,256,L))]),
        in_specs=[V]*4, out_specs=(A,A,V,V,V,V,V),
        scratch_shapes=[pltpu.VMEM((packs,32,2*T),BF),pltpu.VMEM((packs+1,64,T),BF),
            pltpu.VMEM((7,32,L),F32),
            pltpu.SemaphoreType.DMA((2,packs))],
        compiler_params=pltpu.CompilerParams(vmem_limit_bytes=VMEM<<20),
    )(signal,masks,cot,recv)

from jax.sharding import PartitionSpec as P

MESH = pl.DeviceIdType.MESH


def peer(lay, k):
    me = lax.axis_index("dp") * lay.nf + lax.axis_index("fsdp")
    t = lax.rem(me + k, lay.n)
    return me, t, {"dp": t // lay.nf, "fsdp": lax.rem(t, lay.nf)}


def greet(lay):
    barrier = pltpu.get_barrier_semaphore()

    def hello(k, c):
        _, _, dev = peer(lay, k)
        pl.semaphore_signal(barrier, inc=1, device_id=dev, device_id_type=MESH)
        return c

    lax.fori_loop(1, lay.n, hello, 0)
    return barrier


def copy_out(lay, source, recv, send_sem, recv_sem, k):
    me, t, dev = peer(lay, k)
    return pltpu.make_async_remote_copy(
        src_ref=source(t), dst_ref=recv.at[me], send_sem=send_sem.at[k], recv_sem=recv_sem.at[k],
        device_id=dev, device_id_type=MESH)


def send(lay, *args):
    def start(k, c):
        copy_out(lay, *args, k).start()
        return c

    lax.fori_loop(1, lay.n, start, 0)


def receive(lay, *args):
    def finish(k, c):
        copy_out(lay, *args, k).wait()
        return c

    lax.fori_loop(1, lay.n, finish, 0)


def gather_kernel(lay, cot_h, *refs):
    shards_h, seg_h, (out, split, masks), shards = refs[:7], refs[7], refs[8:11], refs[11:18]
    acc, sq, msg, recv, perm, cot, seg, send_sem, recv_sem, in_sem, seg_sem, shard_sem = refs[18:]
    packs, _, width = cot_h.shape
    load = [pltpu.make_async_copy(h, v, shard_sem.at[k]) for k, (h, v) in enumerate(zip(shards_h, shards)) if v.size > 1]
    shards = [h if h.size == 1 else v for h, v in zip(shards_h, shards)]
    fetch = [pltpu.make_async_copy(cot_h.at[p], cot.at[p], in_sem.at[p]) for p in range(packs)]
    barrier = greet(lay)
    count = pltpu.make_async_copy(seg_h, seg, seg_sem)
    for c in load + [count] + fetch:
        c.start()
    acc[...] = jnp.zeros_like(acc)
    sq[...] = jnp.zeros_like(sq)
    for c in load:
        c.wait()
    ud, dd, pd, ug, ub, rg, rb = shards
    for p, o in enumerate(lay.u):
        acc[:, o:o + lay.wu] = ud[8 * p:8 * p + 8].astype(F32)
    for b in range(3):
        acc[:, lay.d[b]:lay.d[b] + lay.wd] = dd[b].astype(F32)
        for j in range(2):
            o = (2 * b + j) * lay.wp
            sq[o:o + lay.wp, 0:8] = pd[b, j].astype(F32)
        o = lay.r[b]
        acc[0:3, o:o + lay.wr] = rg[b].astype(F32)
        acc[3:6, o:o + lay.wr] = rb[b].astype(F32)
    acc[0:1, lay.g:lay.g + lay.wg] = ug[...].astype(F32)
    acc[1:2, lay.g:lay.g + lay.wr] = ub[...].astype(F32)
    full = put(acc[...], sq[...].T[:8], 0, lay.p[0], 6 * lay.wp).astype(BF)
    msg[...] = full
    me = peer(lay, 0)[0]
    recv[me] = full
    step = 8

    def part(p):
        fetch[p].wait()
        for k in range(0, width // (2 * L), step):
            x = jnp.concatenate([cot[p, :, (k + q) * 2 * L:(k + q + 1) * 2 * L] for q in range(step)], axis=0)
            z = dot(x, perm[...]).astype(BF)
            for e in range(2):
                y = jnp.concatenate([z[q * 32:(q + 1) * 32, e * L:(e + 1) * L] for q in range(step)], axis=1)
                split[p, e * 32:(e + 1) * 32, k * L:(k + step) * L] = y

    pl.semaphore_wait(barrier, lay.n - 1)
    args = (lambda t: msg, recv, send_sem, recv_sem)
    send(lay, *args)
    count.wait()
    make_masks(seg, masks, width // (2 * L))
    make_perm(perm, True)
    for p in range(packs):
        part(p)
    receive(lay, *args)
    out[...] = recv[...]


def scatter_kernel(lay, dU, dN, dB, dirs, cols, out, tmp, msgs, recv, send_sem, recv_sem):
    barrier = greet(lay)
    epilogue(lay, dU, dN, dB, dirs, cols, tmp, msgs)
    me = peer(lay, 0)[0]
    recv[me] = msgs[me]
    pl.semaphore_wait(barrier, lay.n - 1)
    args = (lambda t: msgs.at[t], recv, send_sem, recv_sem)
    send(lay, *args)
    receive(lay, *args)
    out[...] = recv[...]


def sum_kernel(lay, recv, gud, gug, gub, gdd, gpd, grg, grb):
    t = recv[0].astype(F32)
    for s in range(1, lay.n):
        t = t + recv[s].astype(F32)
    m = jnp.concatenate([move(t, lay.p[0], 0), jnp.zeros((L - 8, L), F32)], axis=0).T
    for p, o in enumerate(lay.u):
        gud[8 * p:8 * p + 8] = t[:, o:o + lay.wu]
    for b in range(3):
        gdd[b] = t[:, lay.d[b]:lay.d[b] + lay.wd]
        for j in range(2):
            o = (2 * b + j) * lay.wp
            gpd[b, j] = m[o:o + lay.wp, 0:8]
        o = lay.r[b]
        grg[b] = t[0:3, o:o + lay.wr]
        grb[b] = t[3:6, o:o + lay.wr]
    gug[...] = t[0:1, lay.g:lay.g + lay.wg]
    gub[...] = t[1:2, lay.g:lay.g + lay.wr]


def per_device(lay, signal, segments, cotangent, ud, ug, ub, dd, pd, rg, rb):
    V = pl.BlockSpec(memory_space=pltpu.VMEM)
    tiles = jax.ShapeDtypeStruct((lay.n, 8, L), BF)
    sems = [pltpu.SemaphoreType.DMA((lay.n,)), pltpu.SemaphoreType.DMA((lay.n,))]
    packs, _, width = cotangent.shape
    parted = (packs, 64, width // 2)
    H = pl.BlockSpec(memory_space=pltpu.HBM)
    shards = (ud, dd, pd.transpose(0, 1, 3, 2), ug.reshape(1, -1), ub.reshape(1, -1), rg, rb)
    table, split, masks = pl.pallas_call(
        functools.partial(gather_kernel, lay), name="gather_params", out_shape=(tiles, jax.ShapeDtypeStruct(parted, BF), jax.ShapeDtypeStruct((packs * width // (2 * L), 8, 16, L), BF)),
        in_specs=[H] + [H if v.size > 1 else V for v in shards] + [H], out_specs=(V, V, V),
        scratch_shapes=[pltpu.VMEM(v.shape, v.dtype) for v in shards] + [pltpu.VMEM((8, L), F32), pltpu.VMEM((L, L), F32), pltpu.VMEM((8, L), BF), pltpu.VMEM((lay.n, 8, L), BF),
                        pltpu.VMEM((2 * L, 2 * L), BF), pltpu.VMEM(cotangent.shape, BF), pltpu.VMEM(segments.shape, jnp.int32)] + sems
        + [pltpu.SemaphoreType.DMA((packs,)), pltpu.SemaphoreType.DMA, pltpu.SemaphoreType.DMA((7,))],
        compiler_params=pltpu.CompilerParams(collective_id=0, has_side_effects=True, vmem_limit_bytes=20 << 20),
    )(*(pltpu.with_memory_space_constraint(v, pltpu.HBM) if v.size > 1 else v for v in (cotangent, *shards, segments)))
    out, sg, *sums = main_call(NC, lay, signal, masks, split, table)
    got = pl.pallas_call(
        functools.partial(scatter_kernel, lay), name="scatter_grads", out_shape=tiles,
        in_specs=[V] * 5, out_specs=V,
        scratch_shapes=[pltpu.VMEM((6, 32, L), F32), pltpu.VMEM((lay.n, 8, L), BF), pltpu.VMEM((lay.n, 8, L), BF)] + sems,
        compiler_params=pltpu.CompilerParams(collective_id=1, has_side_effects=True, vmem_limit_bytes=4 << 20),
    )(*sums)
    f = lambda *s: jax.ShapeDtypeStruct(s, F32)
    gud, gug, gub, gdd, gpd, grg, grb = pl.pallas_call(
        functools.partial(sum_kernel, lay), name="sum_grads",
        out_shape=(f(*ud.shape), f(1, ug.shape[0]), f(1, ub.shape[0]), f(*dd.shape), f(3, 2, pd.shape[3], pd.shape[2]), f(*rg.shape), f(*rb.shape)),
        in_specs=[V], out_specs=(V,) * 7,
        compiler_params=pltpu.CompilerParams(vmem_limit_bytes=2 << 20),
    )(got)
    return out, sg, gud, gug.reshape(-1), gub.reshape(-1), gdd, gpd.transpose(0, 1, 3, 2), grg, grb


NC = 4


def solution(mesh):
    lay = Lay(mesh.shape["dp"], mesh.shape["fsdp"])
    return jax.shard_map(
        functools.partial(per_device, lay),
        mesh=mesh,
        in_specs=(
            P(("dp", "fsdp"), None, None),
            P(("dp", "fsdp"), None),
            P(("dp", "fsdp"), None, None),
            P("dp", "fsdp"),
            P("fsdp"),
            P("fsdp"),
            P(None, "dp", "fsdp"),
            P(None, None, "dp", "fsdp"),
            P(None, None, "fsdp"),
            P(None, None, "fsdp"),
        ),
        out_specs=(
            P(("dp", "fsdp"), None, None),
            P(("dp", "fsdp"), None, None),
            P("dp", "fsdp"),
            P("fsdp"),
            P("fsdp"),
            P(None, "dp", "fsdp"),
            P(None, None, "dp", "fsdp"),
            P(None, None, "fsdp"),
            P(None, None, "fsdp"),
        ),
        check_vma=False,
    )
```
